32 devices in a mesh: row: 8 (over z, x), off: 4 (over y, core).
Axes of the slice: x: 2, y: 2, z: 4, core: 2. Of those that a mesh axis runs over, the one named last changes fastest.
Arguments:
- start_block: float32 [6, 1048576], P(None, ('row', 'off'))
- diagonal: float32 [1048576], P(('row', 'off')), may hold values from 2 to 6
- tile_values: float32 [8, 4, 80, 128, 128], P('row', 'off'), may hold values from -0.1875 to 0.1875
- tile_rows: int32 [8, 4, 80], P('row', 'off'), may hold values from 0 to 1023
- tile_cols: int32 [8, 4, 80], P('row', 'off'), may hold values from 0 to 1023
- tile_counts: int32 [8, 4], P('row', 'off'), may hold values from 20 to 80, as said below
- offset_map: int32 [4], replicated, may hold values from 0 to 3, as said below
Outputs:
- final_block: float32 [6, 1048576], P(None, ('row', 'off'))
- residual: float32 [6, 1048576], P(None, ('row', 'off'))
The draws below stay inside these ranges and needn't reach their ends.
Inputs may be any that keep to these rules, and one draw needn't show every extreme that they name: `tile_counts`: live tiles of one device; some device has exactly 80. `offset_map`: each offset 0 to 3 is held by 4 / 4 off indices.
All inputs are finite; a program needn't handle non-finite values.
Results may differ from the reference program's by a relative error of at most 0.0003.
Values sent between devices are 32-bit elements; how exact they have to be, the bound alone decides.
No kernel may reach another device: no remote copies, remote signals or barrier semaphores. Data moves between devices by JAX's collectives and lax.ppermute only.
A program may use at most 64 MiB of HBM per device.

```python
import jax
import jax.numpy as jnp
from jax import lax

NV = 6
TILE = 128
TMAX = 80
ITERS = 1
NT = 1024
NTOT = 1048576
N_ROW = 8
N_OFF = 4


def draw_start_block(key, part):
    positions = jnp.arange(NTOT, dtype=jnp.float32) / NTOT
    growth = jnp.exp(jnp.log(3.0) * positions)[None, :]
    sample = jax.random.normal(key, (NV, NTOT), jnp.float32)
    return sample * growth


def draw_tile_counts(key, part):
    sample = jax.random.randint(key, (N_ROW * N_OFF,), max(1, TMAX // 4), TMAX + 1)
    chosen = jax.random.randint(jax.random.fold_in(key, 3), (), 0, N_ROW * N_OFF)
    filled = jnp.where(jnp.arange(N_ROW * N_OFF) == chosen, TMAX, sample)
    return filled.reshape(N_ROW, N_OFF).astype(jnp.int32)


def draw_offset_map(key, part):
    return (jax.random.permutation(key, N_OFF) % (N_ROW // 2)).astype(jnp.int32)


def set_ends(array, own_key, least, top_value):
    spot = [jax.random.randint(jax.random.fold_in(own_key, axis), (), 0, length) for axis, length in enumerate(array.shape)]
    longest = array.shape.index(max(array.shape))
    beside = spot[:longest] + [(spot[longest] + 1) % array.shape[longest]] + spot[longest + 1:]
    return array.at[tuple(spot)].set(least).at[tuple(beside)].set(top_value)


def levels(key, dims, pieces, smallest, high):
    factor_of = 1.0
    for axis_at, parts in pieces:
        steps = jax.random.uniform(jax.random.fold_in(jax.random.fold_in(key, 6), axis_at), (parts,), jnp.float32, smallest / len(pieces), high / len(pieces))
        factor_of = factor_of * jnp.repeat(jnp.exp(steps), dims[axis_at] // parts).reshape((-1,) + (1,) * (len(dims) - 1 - axis_at))
    return factor_of


def scatter_about(key, extent, deviation, limit, pieces=(), kind=jnp.bfloat16):
    drawn = deviation * jax.random.normal(key, extent, jnp.float32)
    if pieces:
        drawn = drawn * levels(key, extent, pieces, -0.22, 0.18)
    return jnp.clip(drawn, -limit, limit).astype(kind)


def setup_inputs(seed: int = 0) -> dict:
    arg_keys = jax.random.split(jax.random.key(seed), 8)
    return {
        "start_block": draw_start_block(jax.random.fold_in(arg_keys[7], 71), 0),
        "diagonal": jnp.clip(2.0 + 4.0 * jax.random.uniform(arg_keys[1], (NTOT,), jnp.float32) ** levels(arg_keys[1], (NTOT,), ((0, 32),), -0.2, 0.2), 2.0, 6.0),
        "tile_values": scatter_about(arg_keys[2], (N_ROW, N_OFF, TMAX, TILE, TILE), 0.03, 0.1875, ((0, 8), (1, 4)), jnp.float32),
        "tile_rows": set_ends(jax.random.randint(arg_keys[3], (N_ROW, N_OFF, TMAX), 0, NT), jax.random.fold_in(arg_keys[3], 1), 0, NT - 1).astype(jnp.int32),
        "tile_cols": set_ends(jax.random.randint(arg_keys[4], (N_ROW, N_OFF, TMAX), 0, NT), jax.random.fold_in(arg_keys[4], 1), 0, NT - 1).astype(jnp.int32),
        "tile_counts": draw_tile_counts(jax.random.fold_in(arg_keys[7], 71), 0),
        "offset_map": draw_offset_map(jax.random.fold_in(arg_keys[7], 71), 0),
    }


HIGH = lax.Precision.HIGHEST

def apply_matrix(block, diagonal, tile_values, tile_rows, tile_cols, tile_counts, offset_map):
    vectors = block.shape[0]
    grouped = block.reshape(vectors, N_ROW, NT, TILE)
    slot_index = jnp.arange(TMAX, dtype=jnp.int32)

    def per_group(group_index):
        col_group = (group_index + offset_map) % N_ROW
        row_ids = tile_rows[group_index]
        col_ids = tile_cols[group_index]
        picked_col = grouped[:, col_group[:, None], col_ids, :]
        picked_row = grouped[:, group_index, row_ids, :]
        tiles = tile_values[group_index]
        live_mask = (slot_index[None, :] < tile_counts[group_index][:, None]).astype(jnp.float32)
        direct = jnp.einsum('votk,otjk->votj', picked_col, tiles, precision=HIGH)
        mirrored = jnp.einsum('votj,otjk->votk', picked_row, tiles, precision=HIGH)
        return (direct * live_mask[None, :, :, None], mirrored * live_mask[None, :, :, None])
    direct_all, mirror_all = lax.map(per_group, jnp.arange(N_ROW, dtype=jnp.int32))
    direct_all = jnp.moveaxis(direct_all, 1, 0)
    mirror_all = jnp.moveaxis(mirror_all, 1, 0)
    group_ids = jnp.broadcast_to(jnp.arange(N_ROW, dtype=jnp.int32)[:, None, None], (N_ROW, N_OFF, TMAX))
    target_groups = (group_ids + offset_map[None, :, None]) % N_ROW
    output = jnp.zeros((vectors, N_ROW, NT, TILE), jnp.float32)
    output = output.at[:, group_ids, tile_rows].add(direct_all)
    output = output.at[:, target_groups, tile_cols].add(mirror_all)
    return output.reshape(vectors, NTOT) + block * diagonal[None, :]

def reference(start_block, diagonal, tile_values, tile_rows, tile_cols, tile_counts, offset_map):
    block = start_block
    residual = start_block
    vectors = block.shape[0]
    for iteration in range(ITERS):
        image = apply_matrix(block, diagonal, tile_values, tile_rows, tile_cols, tile_counts, offset_map)
        gram = jnp.dot(block, block.T, precision=HIGH) / NTOT
        rayleigh = jnp.dot(block, image.T, precision=HIGH) / NTOT
        rayleigh = 0.5 * (rayleigh + rayleigh.T)
        factor = jnp.linalg.cholesky(gram)
        inverse = jax.scipy.linalg.solve_triangular(factor, jnp.eye(vectors, dtype=jnp.float32), lower=True)
        basis = jnp.dot(inverse, block, precision=HIGH)
        applied = jnp.dot(inverse, image, precision=HIGH)
        projected = jnp.dot(jnp.dot(inverse, rayleigh, precision=HIGH), inverse.T, precision=HIGH)
        residual = applied - jnp.dot(projected, basis, precision=HIGH)
        block = basis - residual / diagonal[None, :]
    return (block, residual)
```

```python
import functools

import jax
import jax.numpy as jnp
from jax import lax
from jax.experimental import pallas as pl
from jax.experimental.pallas import tpu as pltpu
from jax.sharding import PartitionSpec as P

HIGH = lax.Precision.HIGHEST
VMEM = pl.BlockSpec(memory_space=pltpu.VMEM)
SMEM = pl.BlockSpec(memory_space=pltpu.SMEM)
MIB = 1 << 20


def swap(x, axis, mask):
    n = lax.axis_size(axis)
    return lax.ppermute(x, axis, [(i, i ^ mask) for i in range(n)])


def shift(x, distance):
    n = lax.axis_size("row")
    return lax.ppermute(x, "row", [(i, (i + distance) % n) for i in range(n)])


def masks_of(n):
    bits = [1 << b for b in reversed(range(n.bit_length() - 1))]
    return bits


def gather_off(x):
    pieces = {0: x}
    for bit in masks_of(lax.axis_size("off")):
        for m in list(pieces):
            pieces[m | bit] = swap(pieces[m], "off", bit)
    return [pieces[m] for m in sorted(pieces)]


def sum_all(x):
    for axis in ("off", "row"):
        bit = 1
        while bit < lax.axis_size(axis):
            x = x + swap(x, axis, bit)
            bit *= 2
    return x


def split(x):
    hi = x.astype(jnp.bfloat16)
    lo = (x - hi.astype(jnp.float32)).astype(jnp.bfloat16)
    return hi, lo


def pick_kernel(vectors, slots, blocks, ids_ref, me_ref, *refs):
    pieces, outs = refs[:-2], refs[-2:]
    me = me_ref[0]
    for which, out in enumerate(outs):

        @pl.loop(0, slots, unroll=4)
        def _(t):
            b = ids_ref[which, t]
            m = jnp.where(b < 0, -1, (jnp.maximum(b, 0) // blocks) ^ me)
            local = jnp.maximum(b, 0) % blocks
            value = jnp.zeros((vectors, out.shape[-1]), jnp.float32)
            for k, piece in enumerate(pieces):
                value = jnp.where(m == k, piece[pl.ds(local, vectors, stride=blocks), :], value)
            out[pl.ds(t, vectors, stride=slots), :] = value


def pick(ids, me, pieces, vectors, slots, blocks):
    width = pieces[0].shape[-1]
    shape = jax.ShapeDtypeStruct((vectors * slots, width), jnp.float32)
    return pl.pallas_call(
        functools.partial(pick_kernel, vectors, slots, blocks),
        out_shape=(shape, shape),
        in_specs=[SMEM, SMEM] + [VMEM] * len(pieces),
        out_specs=(VMEM, VMEM),
        compiler_params=pltpu.CompilerParams(vmem_limit_bytes=12 * MIB),
        name="pick",
    )(ids, me, *pieces)


def multiply_kernel(vectors, slots, step, transposed, x_ref, t_ref, o_ref):
    base = pl.program_id(0) * step
    width = x_ref.shape[-1]
    dims = (((1,), (1 if transposed else 0,)), ((), ()))

    @pl.loop(0, step, unroll=4)
    def _(i):
        t = base + i
        x = x_ref[pl.ds(t, vectors, stride=slots), :]
        x = jnp.concatenate([x, jnp.zeros((8 - vectors, width), jnp.float32)], axis=0)
        hi = x.astype(jnp.bfloat16).astype(jnp.float32)
        both = jnp.concatenate([hi, x - hi], axis=0).astype(jnp.bfloat16)
        t_hi, t_lo = split(t_ref[i])
        a = lax.dot_general(both, t_hi, dims, preferred_element_type=jnp.float32)
        b = lax.dot_general(both, t_lo, dims, preferred_element_type=jnp.float32)
        o_ref[pl.ds(t, vectors, stride=slots), :] = (a[:8] + a[8:] + b[:8])[:vectors]


def multiply(x, tiles, vectors, transposed):
    slots, width, _ = tiles.shape
    step = max(s for s in (1, 2, 4, 8, 16, 20) if slots % s == 0)
    return pl.pallas_call(
        functools.partial(multiply_kernel, vectors, slots, step, transposed),
        out_shape=jax.ShapeDtypeStruct(x.shape, jnp.float32),
        grid=(slots // step,),
        in_specs=[VMEM, pl.BlockSpec((step, width, width), lambda i: (i, 0, 0))],
        out_specs=VMEM,
        compiler_params=pltpu.CompilerParams(vmem_limit_bytes=12 * MIB),
        name="multiply",
    )(x, tiles)


def finish_kernel(vectors, slots, n, inv_ref, a_ref, x_ref, d_ref, ids_ref, *refs):
    lists, (final_ref, residual_ref), (acc, res, fin) = refs[: 2 * n], refs[2 * n : 2 * n + 2], refs[2 * n + 2 :]
    blocks, width = d_ref.shape
    row = lax.broadcasted_iota(jnp.int32, (blocks, slots), 0)
    d = d_ref[...]
    for v in range(vectors):
        acc[pl.ds(v * blocks, blocks), :] = x_ref[pl.ds(v * blocks, blocks), :] * d
    for k in range(2 * n):
        hot = jnp.where(ids_ref[k : k + 1, :slots] == row, 1.0, 0.0).astype(jnp.bfloat16)
        for v in range(vectors):
            hi, lo = split(lists[k][pl.ds(v * slots, slots), :])
            acc[pl.ds(v * blocks, blocks), :] += jnp.dot(
                hot, hi, preferred_element_type=jnp.float32
            ) + jnp.dot(hot, lo, preferred_element_type=jnp.float32)
    rows = 32
    pad = res.shape[0] // vectors

    @pl.loop(0, blocks // rows)
    def _(c):
        at = pl.multiple_of(c * rows, rows)
        xs = [x_ref[pl.ds(v * blocks + at, rows), :] for v in range(vectors)]
        ms = [acc[pl.ds(v * blocks + at, rows), :] for v in range(vectors)]
        dd = 1.0 / d_ref[pl.ds(at, rows), :]
        for i in range(vectors):
            basis = jnp.zeros((rows, width), jnp.float32)
            r = jnp.zeros((rows, width), jnp.float32)
            for j in range(vectors):
                r = r - a_ref[i, j] * xs[j]
            for j in range(i + 1):
                basis = basis + inv_ref[i, j] * xs[j]
                r = r + inv_ref[i, j] * ms[j]
            res[pl.ds(i * pad + at, rows), :] = r
            fin[pl.ds(i * pad + at, rows), :] = basis - r * dd

    @pl.loop(0, blocks, unroll=8)
    def _(b):
        at = pl.multiple_of(b * width, width)
        residual_ref[:, pl.ds(at, width)] = res[pl.ds(b, vectors, stride=pad), :]
        final_ref[:, pl.ds(at, width)] = fin[pl.ds(b, vectors, stride=pad), :]


def finish(inverse, a, packed, diagonal, ids, lists, vectors, slots, shard):
    blocks, width = diagonal.shape
    pad = blocks
    out = jax.ShapeDtypeStruct((vectors, shard), jnp.float32)
    return pl.pallas_call(
        functools.partial(finish_kernel, vectors, slots, len(lists) // 2),
        out_shape=(out, out),
        in_specs=[SMEM, SMEM] + [VMEM] * (3 + len(lists)),
        out_specs=(VMEM, VMEM),
        scratch_shapes=[
            pltpu.VMEM((vectors * blocks, width), jnp.float32),
            pltpu.VMEM((vectors * pad, width), jnp.float32),
            pltpu.VMEM((vectors * pad, width), jnp.float32),
        ],
        compiler_params=pltpu.CompilerParams(vmem_limit_bytes=24 * MIB),
        name="finish",
    )(inverse, a, packed, diagonal, ids, *lists)


def body(start_block, diagonal, tile_values, tile_rows, tile_cols, tile_counts, offset_map):
    tiles = tile_values[0, 0]
    live_count = tile_counts[0, 0]
    row_size = lax.axis_size("row")
    off_size = lax.axis_size("off")
    me = lax.axis_index("off")
    offset = offset_map[me]
    vectors, shard = start_block.shape
    slots, width, _ = tiles.shape
    blocks = shard // width
    total = shard * off_size * row_size
    distances = range(row_size // 2)

    live = jnp.arange(slots, dtype=jnp.int32) < live_count
    row_ids = jnp.where(live, tile_rows[0, 0], -1)
    col_ids = jnp.where(live, tile_cols[0, 0], -1)

    packed = start_block.reshape(vectors * blocks, width)
    pieces = gather_off(packed)

    def padded(ids):
        return jnp.pad(ids[None, :], ((0, 7), (0, 128 - slots)), constant_values=-1)

    group_cols = lax.switch(
        offset,
        [functools.partial(lambda s, c: shift(c, s) if s else c, s) for s in distances],
        padded(col_ids),
    )[0, :slots]
    both = jnp.stack([row_ids, group_cols])
    picked_row, picked_col = pick(
        both, me.astype(jnp.int32)[None], pieces, vectors, slots, blocks
    )
    id_pieces = gather_off(jnp.pad(both, ((0, 6), (0, 128 - slots)), constant_values=-1))

    gram = sum_all(jnp.dot(start_block, start_block.T, precision=HIGH)) / total
    factor = jnp.linalg.cholesky(gram)
    inverse = jax.scipy.linalg.solve_triangular(
        factor, jnp.eye(vectors, dtype=jnp.float32), lower=True
    )
    scaled = jnp.dot(start_block, (start_block * diagonal[None, :]).T, precision=HIGH)

    def middle(s, picked_row, picked_col, tiles):
        arrived = shift(picked_col, -s) if s else picked_col
        mirrored = multiply(picked_row, tiles, vectors, False)
        returned = shift(mirrored, s) if s else mirrored
        direct = multiply(arrived, tiles, vectors, True)
        return direct, returned

    direct, returned = lax.switch(
        offset,
        [functools.partial(middle, s) for s in distances],
        picked_row,
        picked_col,
        tiles,
    )
    cross = jnp.einsum(
        "vtk,wtk->vw",
        returned.reshape(vectors, slots, width),
        picked_col.reshape(vectors, slots, width),
        precision=HIGH,
    )
    rayleigh = sum_all(cross + cross.T + scaled) / total
    direct_lists = gather_off(direct)
    returned_lists = gather_off(returned)
    lists = []
    for a, b in zip(direct_lists, returned_lists):
        lists += [a, b]
    local = jnp.concatenate([p[:2] for p in id_pieces], axis=0) - me * blocks
    projected = jnp.dot(jnp.dot(inverse, rayleigh, precision=HIGH), inverse.T, precision=HIGH)
    onto = jnp.dot(projected, inverse, precision=HIGH)
    return finish(
        inverse,
        onto,
        packed,
        diagonal.reshape(blocks, width),
        local,
        lists,
        vectors,
        slots,
        shard,
    )


def solution(mesh):
    return jax.shard_map(
        body,
        mesh=mesh,
        in_specs=(
            P(None, ("row", "off")),
            P(("row", "off")),
            P("row", "off", None, None, None),
            P("row", "off", None),
            P("row", "off", None),
            P("row", "off"),
            P(),
        ),
        out_specs=(P(None, ("row", "off")), P(None, ("row", "off"))),
        check_vma=False,
    )
```

```python
import functools

import jax
import jax.numpy as jnp
from jax import lax
from jax.experimental import pallas as pl
from jax.experimental.pallas import tpu as pltpu
from jax.sharding import PartitionSpec as P

VMEM = pl.BlockSpec(memory_space=pltpu.VMEM)
SMEM = pl.BlockSpec(memory_space=pltpu.SMEM)
MIB = 1 << 20
BF16 = jnp.bfloat16
F32 = jnp.float32


def swap(x, axis, mask):
    n = lax.axis_size(axis)
    return lax.ppermute(x, axis, [(i, i ^ mask) for i in range(n)])


def shift(x, distance):
    n = lax.axis_size("row")
    return lax.ppermute(x, "row", [(i, (i + distance) % n) for i in range(n)])


def gather_off(x):
    pieces = {0: x}
    bit = lax.axis_size("off") // 2
    while bit:
        for m in list(pieces):
            pieces[m | bit] = swap(pieces[m], "off", bit)
        bit //= 2
    return [pieces[m] for m in sorted(pieces)]


def sum_all(x):
    bit = lax.axis_size("off") // 2
    while bit:
        x = x + swap(x, "off", bit)
        bit //= 2
    bit = 1
    while bit < lax.axis_size("row"):
        x = x + swap(x, "row", bit)
        bit *= 2
    return x


def pairs(vectors):
    return [(i, j) for i in range(vectors) for j in range(i + 1)]


def call(kernel, name, out_shape, operands, in_specs=None, limit=16, scratch=(), flops=0, **kw):
    many = isinstance(out_shape, tuple)
    moved = sum(x.size * x.dtype.itemsize for x in operands)
    return pl.pallas_call(
        kernel,
        out_shape=out_shape,
        in_specs=in_specs or [VMEM] * len(operands),
        out_specs=kw.pop("out_specs", (VMEM,) * len(out_shape) if many else VMEM),
        scratch_shapes=list(scratch),
        compiler_params=pltpu.CompilerParams(vmem_limit_bytes=limit * MIB),
        cost_estimate=pl.CostEstimate(flops=flops, bytes_accessed=moved, transcendentals=0),
        name=name,
        **kw,
    )(*operands)


def pack_kernel(vectors, blocks, x_ref, o_ref):
    width = o_ref.shape[-1]

    @pl.loop(0, blocks, unroll=8)
    def _(b):
        o_ref[pl.ds(b * vectors, vectors), :] = x_ref[:, pl.ds(pl.multiple_of(b * width, width), width)]


def inner_kernel(vectors, x_ref, d_ref, o_ref):
    blocks, width = d_ref.shape
    both = pairs(vectors)
    zero = jnp.zeros((8, width), F32)

    def step(c, sums):
        at = pl.multiple_of(c * 8, 8)
        d = d_ref[pl.ds(at, 8), :]
        x = [x_ref[pl.ds(at * vectors + v, 8, stride=vectors), :] for v in range(vectors)]
        y = [a * d for a in x]
        first = [s + x[i] * x[j] for s, (i, j) in zip(sums, both)]
        second = [s + x[i] * y[j] for s, (i, j) in zip(sums[len(both) :], both)]
        return tuple(first + second)

    sums = lax.fori_loop(0, blocks // 8, step, (zero,) * (2 * len(both)))
    for k, s in enumerate(sums):
        o_ref[pl.ds(8 * k, 8), :] = s


def divide_kernel(t_ref, hi_ref, lo_ref):
    t = t_ref[...]
    hi = t.astype(BF16)
    hi_ref[...] = hi
    lo_ref[...] = (t - hi.astype(F32)).astype(BF16)


def divide(tiles):
    slots, width, _ = tiles.shape
    step = max(s for s in (1, 2, 4, 8) if slots % s == 0)
    spec = pl.BlockSpec((step, width, width), lambda i: (i, 0, 0))
    shape = jax.ShapeDtypeStruct(tiles.shape, BF16)
    return call(
        divide_kernel, "divide", (shape, shape), (tiles,), [spec], 8,
        flops=tiles.size * 4, grid=(slots // step,), out_specs=(spec, spec),
    )


def pick_kernel(vectors, slots, where_ref, at_ref, *refs):
    pieces, outs = refs[:-2], refs[-2:]
    for which, out in enumerate(outs):

        @pl.loop(0, slots, unroll=4)
        def _(t):
            m = where_ref[which, t]
            at = at_ref[which, t]
            value = jnp.zeros((vectors, out.shape[-1]), F32)
            for k, piece in enumerate(pieces):
                value = jnp.where(m == k, piece[pl.ds(at, vectors), :], value)
            out[pl.ds(t * vectors, vectors), :] = value


def multiply_kernel(vectors, step, transposed, x_ref, hi_ref, lo_ref, o_ref):
    base = pl.program_id(0) * step
    width = x_ref.shape[-1]
    dims = (((1,), (1 if transposed else 0,)), ((), ()))

    def left(t):
        x = x_ref[pl.ds(t * vectors, vectors), :]
        x = jnp.concatenate([x, jnp.zeros((8 - vectors, width), F32)], axis=0)
        hi = x.astype(BF16).astype(F32)
        lo = x - hi
        top = jnp.concatenate([hi, hi], axis=1)
        low = jnp.concatenate([lo, jnp.zeros_like(lo)], axis=1)
        return [top, low]

    @pl.loop(0, step // 2, unroll=2)
    def _(p):
        i = 2 * p
        x = jnp.concatenate(left(base + i) + left(base + i + 1), axis=0).astype(BF16)
        a, b = 0, 1
        if transposed:
            t = [jnp.concatenate([hi_ref[i + k], lo_ref[i + k]], axis=1) for k in (a, b)]
            t = jnp.concatenate(t, axis=0)
        else:
            t = [jnp.concatenate([hi_ref[i + k], lo_ref[i + k]], axis=0) for k in (a, b)]
            t = jnp.concatenate(t, axis=1)
        y = lax.dot_general(x, t, dims, preferred_element_type=F32)
        o_ref[pl.ds((base + i) * vectors, vectors), :] = (y[0:8, :width] + y[8:16, :width])[:vectors]
        o_ref[pl.ds((base + i + 1) * vectors, vectors), :] = (y[16:24, width:] + y[24:32, width:])[:vectors]


def multiply(x, high, low, ids, vectors, transposed):
    slots, width, _ = high.shape
    step = max(s for s in (2, 4, 8, 16, 20) if slots % s == 0)
    rows = vectors * slots
    spec = pl.BlockSpec((step, width, width), lambda i: (i, 0, 0))

    def kernel(x_ref, hi_ref, lo_ref, ids_ref, o_ref):
        multiply_kernel(vectors, step, transposed, x_ref, hi_ref, lo_ref, o_ref)
        o_ref[pl.ds(rows, 8), :] = ids_ref[...]

    return call(
        kernel, "multiply", jax.ShapeDtypeStruct((rows + 8, width), F32), (x, high, low, ids),
        [VMEM, spec, spec, VMEM], 12, flops=slots * 2 * 32 * 256 * 128, grid=(slots // step,), out_specs=VMEM,
    )


def couple_kernel(vectors, slots, x_ref, y_ref, p_ref, o_ref):
    both = pairs(vectors)
    n = len(both)
    sums = [p_ref[pl.ds(8 * (n + k), 8), :] for k in range(n)]
    for c in range(slots // 8):
        x = [x_ref[pl.ds(8 * c * vectors + v, 8, stride=vectors), :] for v in range(vectors)]
        y = [y_ref[pl.ds(8 * c * vectors + v, 8, stride=vectors), :] for v in range(vectors)]
        sums = [s + (x[i] * y[j] + x[j] * y[i]) for s, (i, j) in zip(sums, both)]
    sums = [p_ref[pl.ds(8 * k, 8), :] for k in range(n)] + sums
    for k, s in enumerate(sums):
        o_ref[k : k + 1, :] = jnp.sum(s, axis=0, keepdims=True)
    if o_ref.shape[0] > 2 * n:
        o_ref[2 * n :, :] = jnp.zeros((o_ref.shape[0] - 2 * n, o_ref.shape[1]), F32)
    total = jnp.sum(o_ref[...], axis=1, keepdims=True)
    o_ref[...] = jnp.broadcast_to(total, o_ref.shape)


def add_kernel(vectors, slots, blocks, started, me_ref, *refs):
    o_ref, lists = refs[-1], refs[:-1]
    if started:
        before, lists = lists[0], lists[1:]
    width = o_ref.shape[-1]
    row = lax.broadcasted_iota(jnp.int32, (blocks, width), 0) + me_ref[0] * blocks
    row = row.astype(F32)
    pad = jnp.zeros((width - slots, vectors * width), F32)
    sums = None
    for k in range(0, len(lists), 2):
        hots, blocks_of = [], []
        for ref in lists[k : k + 2]:
            ids = ref[vectors * slots : vectors * slots + 1, :]
            hots.append(jnp.where(ids == row, 1.0, 0.0).astype(BF16))
            y = [ref[pl.ds(v, slots, stride=vectors), :] for v in range(vectors)]
            blocks_of += [jnp.concatenate(y, axis=1), pad]
        hot = jnp.concatenate(hots, axis=1)
        y = jnp.concatenate(blocks_of, axis=0)
        hi = y.astype(BF16)
        lo = (y - hi.astype(F32)).astype(BF16)
        part = jnp.dot(hot, hi, preferred_element_type=F32) + jnp.dot(hot, lo, preferred_element_type=F32)
        sums = part if sums is None else sums + part
    for v in range(vectors):
        s = sums[:, v * width : (v + 1) * width]
        if started:
            s = s + before[pl.ds(v * blocks, blocks), :]
        o_ref[pl.ds(v * blocks, blocks), :] = s


def add_lists(me, lists, vectors, slots, blocks, before=None):
    width = lists[0].shape[-1]
    operands = (me,) + (() if before is None else (before,)) + tuple(lists)
    return call(
        functools.partial(add_kernel, vectors, slots, blocks, before is not None),
        "add_lists", jax.ShapeDtypeStruct((vectors * blocks, width), F32), operands,
        [SMEM] + [VMEM] * (len(operands) - 1), 16, flops=len(lists) * 2 * 256 * 256 * 768,
    )


def algebra(vectors, total, sums_ref):
    both = pairs(vectors)
    n = len(both)
    g, q = {}, {}
    for k, (i, j) in enumerate(both):
        g[i, j] = sums_ref[k : k + 1, :] * (1.0 / total)
        q[i, j] = q[j, i] = sums_ref[n + k : n + k + 1, :] * (1.0 / total)
    low, inv = {}, {}
    rev = []
    for j in range(vectors):
        s = g[j, j]
        for k in range(j):
            s = s - low[j, k] * low[j, k]
        rev.append(1.0 / jnp.sqrt(s))
        for i in range(j + 1, vectors):
            s = g[i, j]
            for k in range(j):
                s = s - low[i, k] * low[j, k]
            low[i, j] = s * rev[j]
    for j in range(vectors):
        inv[j, j] = rev[j]
        for i in range(j + 1, vectors):
            s = low[i, j] * inv[j, j]
            for k in range(j + 1, i):
                s = s + low[i, k] * inv[k, j]
            inv[i, j] = -s * rev[i]
    half, onto, proj = {}, {}, {}
    for i in range(vectors):
        for j in range(vectors):
            half[i, j] = sum(inv[i, k] * q[k, j] for k in range(i + 1))
    for i in range(vectors):
        for j in range(vectors):
            proj[i, j] = sum(half[i, k] * inv[j, k] for k in range(j + 1))
    for i in range(vectors):
        for j in range(vectors):
            onto[i, j] = sum(proj[i, k] * inv[k, j] for k in range(j, vectors))
    return inv, onto


def finish_kernel(vectors, total, sums_ref, x_ref, d_ref, m_ref, final_ref, residual_ref, coef, res, fin):
    blocks, width = d_ref.shape
    inv, onto = algebra(vectors, total, sums_ref)
    places = {}
    for name, table in (("i", inv), ("o", onto)):
        for key in sorted(table):
            k = len(places)
            places[name, key] = k
            coef[pl.ds(8 * k, 8), :] = jnp.broadcast_to(table[key], (8, width))

    @pl.loop(0, blocks // 8, unroll=2)
    def _(c):
        at = pl.multiple_of(c * 8, 8)
        d = d_ref[pl.ds(at, 8), :]
        rd = 1.0 / d
        x = [x_ref[pl.ds(at * vectors + v, 8, stride=vectors), :] for v in range(vectors)]
        m = [m_ref[pl.ds(v * blocks + at, 8), :] + x[v] * d for v in range(vectors)]

        def value(name, i, j):
            return coef[pl.ds(8 * places[name, (i, j)], 8), :]

        for i in range(vectors):
            basis = r = None
            for j in range(i + 1):
                f = value("i", i, j)
                basis = f * x[j] if basis is None else basis + f * x[j]
                r = f * m[j] if r is None else r + f * m[j]
            for j in range(vectors):
                r = r - value("o", i, j) * x[j]
            res[pl.ds(8 * at + i, 8, stride=8), :] = r
            fin[pl.ds(8 * at + i, 8, stride=8), :] = basis - r * rd

    @pl.loop(0, blocks, unroll=8)
    def _(b):
        at = pl.multiple_of(b * width, width)
        residual_ref[:, pl.ds(at, width)] = res[pl.ds(pl.multiple_of(8 * b, 8), vectors), :]
        final_ref[:, pl.ds(at, width)] = fin[pl.ds(pl.multiple_of(8 * b, 8), vectors), :]


def body(start_block, diagonal, tile_values, tile_rows, tile_cols, tile_counts, offset_map):
    tiles = tile_values[0, 0]
    live_count = tile_counts[0, 0]
    row_size = lax.axis_size("row")
    off_size = lax.axis_size("off")
    me = lax.axis_index("off").astype(jnp.int32)
    offset = offset_map[me]
    vectors, shard = start_block.shape
    slots, width, _ = tiles.shape
    blocks = shard // width
    total = shard * off_size * row_size
    distances = range(row_size // 2)
    count = len(pairs(vectors))

    packed = call(
        functools.partial(pack_kernel, vectors, blocks), "pack",
        jax.ShapeDtypeStruct((vectors * blocks, width), F32), (start_block,),
    )
    pieces = gather_off(packed)

    live = jnp.arange(slots, dtype=jnp.int32) < live_count
    row_ids = jnp.where(live, tile_rows[0, 0], -1)
    col_ids = jnp.where(live, tile_cols[0, 0], -1)

    def padded(ids):
        return jnp.pad(ids.astype(F32)[None, :], ((0, 7), (0, width - slots)), constant_values=-1)

    row_line, col_line = padded(row_ids), padded(col_ids)
    group_line = lax.switch(
        offset,
        [functools.partial(lambda s, c: shift(c, s) if s else c, s) for s in distances],
        col_line,
    )
    both = jnp.stack([row_ids, group_line[0, :slots].astype(jnp.int32)])
    where = jnp.where(both < 0, -1, (both // blocks) ^ me)
    at = jnp.where(both < 0, 0, both % blocks) * vectors

    diagonal = diagonal.reshape(blocks, width)
    inner = call(
        functools.partial(inner_kernel, vectors), "inner",
        jax.ShapeDtypeStruct((16 * count, width), F32), (packed, diagonal),
    )
    high, low = divide(tiles)
    picked = jax.ShapeDtypeStruct((vectors * slots, width), F32)
    picked_row, picked_col = call(
        functools.partial(pick_kernel, vectors, slots), "pick", (picked, picked),
        (where, at, *pieces), [SMEM, SMEM] + [VMEM] * off_size,
    )

    def middle(s, picked_row, picked_col, high, low, row_line, col_line):
        arrived = shift(picked_col, -s) if s else picked_col
        mirrored = multiply(picked_row, high, low, col_line, vectors, False)
        returned = shift(mirrored, s) if s else mirrored
        direct = multiply(arrived, high, low, row_line, vectors, True)
        return direct, returned

    direct, returned = lax.switch(
        offset,
        [functools.partial(middle, s) for s in distances],
        picked_row, picked_col, high, low, row_line, col_line,
    )
    sums = call(
        functools.partial(couple_kernel, vectors, slots), "couple",
        jax.ShapeDtypeStruct((-(-2 * count // 8) * 8, width), F32), (picked_row, direct, inner),
    )
    sums = sum_all(sums)
    lists = []
    for a, b in zip(gather_off(direct), gather_off(returned)):
        lists += [a, b]
    half = off_size
    image = add_lists(me[None], lists[:half], vectors, slots, blocks)
    image = add_lists(me[None], lists[half:], vectors, slots, blocks, image)
    out = jax.ShapeDtypeStruct((vectors, shard), F32)
    return call(
        functools.partial(finish_kernel, vectors, float(total)), "finish", (out, out),
        (sums, packed, diagonal, image), limit=24,
        scratch=(
            pltpu.VMEM((8 * (vectors * vectors + count), width), F32),
            pltpu.VMEM((8 * blocks, width), F32),
            pltpu.VMEM((8 * blocks, width), F32),
        ),
    )


def solution(mesh):
    return jax.shard_map(
        body,
        mesh=mesh,
        in_specs=(
            P(None, ("row", "off")),
            P(("row", "off")),
            P("row", "off", None, None, None),
            P("row", "off", None),
            P("row", "off", None),
            P("row", "off"),
            P(),
        ),
        out_specs=(P(None, ("row", "off")), P(None, ("row", "off"))),
        check_vma=False,
    )
```

```python
import functools

import jax
import jax.numpy as jnp
from jax import lax
from jax.experimental import pallas as pl
from jax.experimental.pallas import tpu as pltpu
from jax.sharding import PartitionSpec as P

VMEM = pl.BlockSpec(memory_space=pltpu.VMEM)
SMEM = pl.BlockSpec(memory_space=pltpu.SMEM)
MIB = 1 << 20
BF16 = jnp.bfloat16
F32 = jnp.float32


def swap(x, axis, mask):
    n = lax.axis_size(axis)
    return lax.ppermute(x, axis, [(i, i ^ mask) for i in range(n)])


def shift(x, distance):
    n = lax.axis_size("row")
    return lax.ppermute(x, "row", [(i, (i + distance) % n) for i in range(n)])


def after(x, *others):
    return lax.optimization_barrier((x, *others))[0]


def bits_of(axis):
    return [1 << b for b in reversed(range(lax.axis_size(axis).bit_length() - 1))]


def gather_off(x, name, hold=()):
    pieces = {0: x}
    for level, bit in enumerate(bits_of("off")):
        for m in list(pieces):
            with jax.named_scope(f"{name}_{level}_{m}"):
                source = after(pieces[m], *hold) if m and hold else pieces[m]
                pieces[m | bit] = swap(source, "off", bit)
    return [pieces[m] for m in sorted(pieces)]


def sum_step(x, axis, bit, name):
    with jax.named_scope(name):
        return x + swap(x, axis, bit)


def pairs(vectors):
    return [(i, j) for i in range(vectors) for j in range(i + 1)]


def call(kernel, name, out_shape, operands, in_specs=None, limit=16, scratch=(), flops=0, **kw):
    many = isinstance(out_shape, tuple)
    moved = sum(x.size * x.dtype.itemsize for x in operands)
    return pl.pallas_call(
        kernel,
        out_shape=out_shape,
        in_specs=in_specs or [VMEM] * len(operands),
        out_specs=kw.pop("out_specs", (VMEM,) * len(out_shape) if many else VMEM),
        scratch_shapes=list(scratch),
        compiler_params=pltpu.CompilerParams(vmem_limit_bytes=limit * MIB),
        cost_estimate=pl.CostEstimate(flops=flops, bytes_accessed=moved, transcendentals=0),
        name=name,
        **kw,
    )(*operands)


def pack_kernel(vectors, blocks, x_ref, o_ref):
    width = o_ref.shape[-1]

    @pl.loop(0, blocks, unroll=8)
    def _(b):
        o_ref[pl.ds(b * vectors, vectors), :] = x_ref[:, pl.ds(pl.multiple_of(b * width, width), width)]


def inner_kernel(vectors, x_ref, d_ref, o_ref):
    blocks, width = d_ref.shape
    both = pairs(vectors)
    zero = jnp.zeros((8, width), F32)

    def step(c, sums):
        at = pl.multiple_of(c * 8, 8)
        d = d_ref[pl.ds(at, 8), :]
        x = [x_ref[pl.ds(at * vectors + v, 8, stride=vectors), :] for v in range(vectors)]
        y = [a * d for a in x]
        first = [s + x[i] * x[j] for s, (i, j) in zip(sums, both)]
        second = [s + x[i] * y[j] for s, (i, j) in zip(sums[len(both) :], both)]
        return tuple(first + second)

    sums = lax.fori_loop(0, blocks // 8, step, (zero,) * (2 * len(both)))
    for k, s in enumerate(sums):
        o_ref[pl.ds(8 * k, 8), :] = s


def divide_kernel(t_ref, hi_ref, lo_ref):
    t = t_ref[...]
    hi = t.astype(BF16)
    hi_ref[...] = hi
    lo_ref[...] = (t - hi.astype(F32)).astype(BF16)


def divide(tiles):
    slots, width, _ = tiles.shape
    step = max(s for s in (1, 2, 4, 8) if slots % s == 0)
    spec = pl.BlockSpec((step, width, width), lambda i: (i, 0, 0))
    shape = jax.ShapeDtypeStruct(tiles.shape, BF16)
    return call(
        divide_kernel, "divide", (shape, shape), (tiles,), [spec], 8,
        flops=tiles.size * 4, grid=(slots // step,), out_specs=(spec, spec),
    )


def pick_kernel(vectors, slots, where_ref, at_ref, *refs):
    pieces, outs = refs[:-2], refs[-2:]
    for which, out in enumerate(outs):

        @pl.loop(0, slots, unroll=4)
        def _(t):
            m = where_ref[which, t]
            at = at_ref[which, t]
            value = jnp.zeros((vectors, out.shape[-1]), F32)
            for k, piece in enumerate(pieces):
                value = jnp.where(m == k, piece[pl.ds(at, vectors), :], value)
            out[pl.ds(t * vectors, vectors), :] = value


def multiply_kernel(vectors, step, transposed, x_ref, hi_ref, lo_ref, o_ref):
    base = pl.program_id(0) * step
    width = x_ref.shape[-1]
    dims = (((1,), (1 if transposed else 0,)), ((), ()))

    def left(t):
        x = x_ref[pl.ds(t * vectors, vectors), :]
        x = jnp.concatenate([x, jnp.zeros((8 - vectors, width), F32)], axis=0)
        hi = x.astype(BF16).astype(F32)
        lo = x - hi
        top = jnp.concatenate([hi, hi], axis=1)
        low = jnp.concatenate([lo, jnp.zeros_like(lo)], axis=1)
        return [top, low]

    @pl.loop(0, step // 2, unroll=2)
    def _(p):
        i = 2 * p
        x = jnp.concatenate(left(base + i) + left(base + i + 1), axis=0).astype(BF16)
        a, b = 0, 1
        if transposed:
            t = [jnp.concatenate([hi_ref[i + k], lo_ref[i + k]], axis=1) for k in (a, b)]
            t = jnp.concatenate(t, axis=0)
        else:
            t = [jnp.concatenate([hi_ref[i + k], lo_ref[i + k]], axis=0) for k in (a, b)]
            t = jnp.concatenate(t, axis=1)
        y = lax.dot_general(x, t, dims, preferred_element_type=F32)
        o_ref[pl.ds((base + i) * vectors, vectors), :] = (y[0:8, :width] + y[8:16, :width])[:vectors]
        o_ref[pl.ds((base + i + 1) * vectors, vectors), :] = (y[16:24, width:] + y[24:32, width:])[:vectors]


def multiply(x, high, low, ids, vectors, transposed):
    slots, width, _ = high.shape
    step = max(s for s in (2, 4, 8, 16, 20) if slots % s == 0)
    rows = vectors * slots
    spec = pl.BlockSpec((step, width, width), lambda i: (i, 0, 0))

    def kernel(x_ref, hi_ref, lo_ref, ids_ref, o_ref):
        multiply_kernel(vectors, step, transposed, x_ref, hi_ref, lo_ref, o_ref)
        o_ref[pl.ds(rows, 8), :] = ids_ref[...]

    return call(
        kernel, "multiply", jax.ShapeDtypeStruct((rows + 8, width), F32), (x, high, low, ids),
        [VMEM, spec, spec, VMEM], 12, flops=slots * 2 * 32 * 256 * 128, grid=(slots // step,), out_specs=VMEM,
    )


def couple_kernel(vectors, slots, x_ref, y_ref, p_ref, o_ref):
    both = pairs(vectors)
    n = len(both)
    sums = [p_ref[pl.ds(8 * (n + k), 8), :] for k in range(n)]
    for c in range(slots // 8):
        x = [x_ref[pl.ds(8 * c * vectors + v, 8, stride=vectors), :] for v in range(vectors)]
        y = [y_ref[pl.ds(8 * c * vectors + v, 8, stride=vectors), :] for v in range(vectors)]
        sums = [s + (x[i] * y[j] + x[j] * y[i]) for s, (i, j) in zip(sums, both)]
    sums = [p_ref[pl.ds(8 * k, 8), :] for k in range(n)] + sums
    for k, s in enumerate(sums):
        o_ref[k : k + 1, :] = jnp.sum(s, axis=0, keepdims=True)
    if o_ref.shape[0] > 2 * n:
        o_ref[2 * n :, :] = jnp.zeros((o_ref.shape[0] - 2 * n, o_ref.shape[1]), F32)
    total = jnp.sum(o_ref[...], axis=1, keepdims=True)
    o_ref[...] = jnp.broadcast_to(total, o_ref.shape)


def add_kernel(vectors, slots, blocks, started, me_ref, *refs):
    o_ref, lists = refs[-1], refs[:-1]
    if started:
        before, lists = lists[0], lists[1:]
    width = o_ref.shape[-1]
    row = lax.broadcasted_iota(jnp.int32, (blocks, width), 0) + me_ref[0] * blocks
    row = row.astype(F32)
    pad = jnp.zeros((width - slots, vectors * width), F32)
    sums = None
    for k in range(0, len(lists), 2):
        hots, blocks_of = [], []
        for ref in lists[k : k + 2]:
            ids = ref[vectors * slots : vectors * slots + 1, :]
            hots.append(jnp.where(ids == row, 1.0, 0.0).astype(BF16))
            y = [ref[pl.ds(v, slots, stride=vectors), :] for v in range(vectors)]
            blocks_of += [jnp.concatenate(y, axis=1), pad]
        hot = jnp.concatenate(hots, axis=1)
        y = jnp.concatenate(blocks_of, axis=0)
        hi = y.astype(BF16)
        lo = (y - hi.astype(F32)).astype(BF16)
        part = jnp.dot(hot, hi, preferred_element_type=F32) + jnp.dot(hot, lo, preferred_element_type=F32)
        sums = part if sums is None else sums + part
    for v in range(vectors):
        s = sums[:, v * width : (v + 1) * width]
        if started:
            s = s + before[pl.ds(v * blocks, blocks), :]
        o_ref[pl.ds(v * blocks, blocks), :] = s


def add_lists(me, lists, vectors, slots, blocks, before=None):
    width = lists[0].shape[-1]
    operands = (me,) + (() if before is None else (before,)) + tuple(lists)
    return call(
        functools.partial(add_kernel, vectors, slots, blocks, before is not None),
        "add_lists", jax.ShapeDtypeStruct((vectors * blocks, width), F32), operands,
        [SMEM] + [VMEM] * (len(operands) - 1), 16, flops=len(lists) * 2 * 256 * 256 * 768,
    )


def algebra(vectors, total, sums_ref):
    both = pairs(vectors)
    n = len(both)
    g, q = {}, {}
    for k, (i, j) in enumerate(both):
        g[i, j] = sums_ref[k : k + 1, :] * (1.0 / total)
        q[i, j] = q[j, i] = sums_ref[n + k : n + k + 1, :] * (1.0 / total)
    low, inv = {}, {}
    rev = []
    for j in range(vectors):
        s = g[j, j]
        for k in range(j):
            s = s - low[j, k] * low[j, k]
        rev.append(1.0 / jnp.sqrt(s))
        for i in range(j + 1, vectors):
            s = g[i, j]
            for k in range(j):
                s = s - low[i, k] * low[j, k]
            low[i, j] = s * rev[j]
    for j in range(vectors):
        inv[j, j] = rev[j]
        for i in range(j + 1, vectors):
            s = low[i, j] * inv[j, j]
            for k in range(j + 1, i):
                s = s + low[i, k] * inv[k, j]
            inv[i, j] = -s * rev[i]
    half, onto, proj = {}, {}, {}
    for i in range(vectors):
        for j in range(vectors):
            half[i, j] = sum(inv[i, k] * q[k, j] for k in range(i + 1))
    for i in range(vectors):
        for j in range(vectors):
            proj[i, j] = sum(half[i, k] * inv[j, k] for k in range(j + 1))
    for i in range(vectors):
        for j in range(vectors):
            onto[i, j] = sum(proj[i, k] * inv[k, j] for k in range(j, vectors))
    return inv, onto


def finish_kernel(vectors, total, sums_ref, x_ref, d_ref, m_ref, final_ref, residual_ref, coef, res, fin):
    blocks, width = d_ref.shape
    inv, onto = algebra(vectors, total, sums_ref)
    places = {}
    for name, table in (("i", inv), ("o", onto)):
        for key in sorted(table):
            k = len(places)
            places[name, key] = k
            coef[pl.ds(8 * k, 8), :] = jnp.broadcast_to(table[key], (8, width))

    @pl.loop(0, blocks // 8, unroll=2)
    def _(c):
        at = pl.multiple_of(c * 8, 8)
        d = d_ref[pl.ds(at, 8), :]
        rd = 1.0 / d
        x = [x_ref[pl.ds(at * vectors + v, 8, stride=vectors), :] for v in range(vectors)]
        m = [m_ref[pl.ds(v * blocks + at, 8), :] + x[v] * d for v in range(vectors)]

        def value(name, i, j):
            return coef[pl.ds(8 * places[name, (i, j)], 8), :]

        for i in range(vectors):
            basis = r = None
            for j in range(i + 1):
                f = value("i", i, j)
                basis = f * x[j] if basis is None else basis + f * x[j]
                r = f * m[j] if r is None else r + f * m[j]
            for j in range(vectors):
                r = r - value("o", i, j) * x[j]
            res[pl.ds(8 * at + i, 8, stride=8), :] = r
            fin[pl.ds(8 * at + i, 8, stride=8), :] = basis - r * rd

    @pl.loop(0, blocks, unroll=8)
    def _(b):
        at = pl.multiple_of(b * width, width)
        residual_ref[:, pl.ds(at, width)] = res[pl.ds(pl.multiple_of(8 * b, 8), vectors), :]
        final_ref[:, pl.ds(at, width)] = fin[pl.ds(pl.multiple_of(8 * b, 8), vectors), :]


def body(start_block, diagonal, tile_values, tile_rows, tile_cols, tile_counts, offset_map):
    tiles = tile_values[0, 0]
    live_count = tile_counts[0, 0]
    row_size = lax.axis_size("row")
    off_size = lax.axis_size("off")
    me = lax.axis_index("off").astype(jnp.int32)
    offset = offset_map[me]
    vectors, shard = start_block.shape
    slots, width, _ = tiles.shape
    blocks = shard // width
    total = shard * off_size * row_size
    distances = range(row_size // 2)
    count = len(pairs(vectors))

    packed = call(
        functools.partial(pack_kernel, vectors, blocks), "pack",
        jax.ShapeDtypeStruct((vectors * blocks, width), F32), (start_block,),
    )
    live = jnp.arange(slots, dtype=jnp.int32) < live_count
    row_ids = jnp.where(live, tile_rows[0, 0], -1)
    col_ids = jnp.where(live, tile_cols[0, 0], -1)

    def padded(ids):
        return jnp.pad(ids.astype(F32)[None, :], ((0, 7), (0, width - slots)), constant_values=-1)

    row_line, col_line = padded(row_ids), padded(col_ids)
    group_line = lax.switch(
        offset,
        [functools.partial(lambda s, c: shift(c, s) if s else c, s) for s in distances],
        col_line,
    )
    both = jnp.stack([row_ids, group_line[0, :slots].astype(jnp.int32)])
    where = jnp.where(both < 0, -1, (both // blocks) ^ me)
    at = jnp.where(both < 0, 0, both % blocks) * vectors

    diagonal = diagonal.reshape(blocks, width)
    inner = call(
        functools.partial(inner_kernel, vectors), "inner",
        jax.ShapeDtypeStruct((16 * count, width), F32), (packed, diagonal),
    )
    high, low = divide(tiles)
    pieces = gather_off(packed, "pieces", (where, at, inner, high, low))
    picked = jax.ShapeDtypeStruct((vectors * slots, width), F32)
    picked_row, picked_col = call(
        functools.partial(pick_kernel, vectors, slots), "pick", (picked, picked),
        (where, at, *pieces), [SMEM, SMEM] + [VMEM] * off_size,
    )

    row_bits, off_bits = bits_of("row")[::-1], bits_of("off")[::-1]

    def middle(s, picked_row, picked_col, high, low, row_line, col_line, inner):
        with jax.named_scope("columns"):
            arrived = shift(picked_col, -s) if s else picked_col
        mirrored = multiply(picked_row, high, low, col_line, vectors, False)
        with jax.named_scope("products"):
            returned = shift(mirrored, s) if s else mirrored
        direct = multiply(arrived, high, low, row_line, vectors, True)
        sums = call(
            functools.partial(couple_kernel, vectors, slots), "couple",
            jax.ShapeDtypeStruct((-(-2 * count // 8) * 8, width), F32), (picked_row, direct, inner),
        )
        sums = sum_step(sums, "row", row_bits[0], "first")
        return direct, returned, sums

    direct, returned, sums = lax.switch(
        offset,
        [functools.partial(middle, s) for s in distances],
        picked_row, picked_col, high, low, row_line, col_line, inner,
    )
    stages = [sums]
    for k, (axis, bit) in enumerate([("row", b) for b in row_bits[1:]] + [("off", b) for b in off_bits]):
        stages.append(sum_step(stages[-1], axis, bit, f"sum_{k}"))
    sums = stages[-1]
    late = len(row_bits) - 1
    lists = []
    for a, b in zip(
        gather_off(direct, "direct", (stages[late],)), gather_off(returned, "returned", (stages[late + 1],))
    ):
        lists += [a, b]
    half = off_size
    image = add_lists(me[None], lists[:half], vectors, slots, blocks)
    image = add_lists(me[None], lists[half:], vectors, slots, blocks, image)
    out = jax.ShapeDtypeStruct((vectors, shard), F32)
    return call(
        functools.partial(finish_kernel, vectors, float(total)), "finish", (out, out),
        (sums, packed, diagonal, image), limit=24,
        scratch=(
            pltpu.VMEM((8 * (vectors * vectors + count), width), F32),
            pltpu.VMEM((8 * blocks, width), F32),
            pltpu.VMEM((8 * blocks, width), F32),
        ),
    )


def solution(mesh):
    return jax.shard_map(
        body,
        mesh=mesh,
        in_specs=(
            P(None, ("row", "off")),
            P(("row", "off")),
            P("row", "off", None, None, None),
            P("row", "off", None),
            P("row", "off", None),
            P("row", "off"),
            P(),
        ),
        out_specs=(P(None, ("row", "off")), P(None, ("row", "off"))),
        check_vma=False,
    )
```

```python
import functools
import itertools

import jax
import jax.numpy as jnp
from jax import lax
from jax.experimental import pallas as pl
from jax.experimental.pallas import tpu as pltpu
from jax.sharding import PartitionSpec as P


VMEM = pl.BlockSpec(memory_space=pltpu.VMEM)
SMEM = pl.BlockSpec(memory_space=pltpu.SMEM)
MIB = 1 << 20
BF16 = jnp.bfloat16
F32 = jnp.float32


def swap(x, axis, mask):
    n = lax.axis_size(axis)
    return lax.ppermute(x, axis, [(i, i ^ mask) for i in range(n)])


def shift(x, distances):
    rows, offs = lax.axis_size("row"), lax.axis_size("off")
    if not any(distances):
        return x
    route = [
        (r * offs + o, (r + distances[o]) % rows * offs + o) for r in range(rows) for o in range(offs)
    ]
    return lax.ppermute(x, ("row", "off"), route)


def after(x, *others):
    return lax.optimization_barrier((x, *others))[0]


def bits_of(axis):
    return [1 << b for b in reversed(range(lax.axis_size(axis).bit_length() - 1))]


def gather_off(pieces, bits, hold=()):
    pieces = dict(pieces)
    for bit in bits:
        for m in list(pieces):
            source = after(pieces[m], *hold) if m and hold else pieces[m]
            pieces[m | bit] = swap(source, "off", bit)
    return [pieces[m] for m in sorted(pieces)]


def sum_step(x, axis, bit):
    return x + swap(x, axis, bit)


def pairs(vectors):
    return [(i, j) for i in range(vectors) for j in range(i + 1)]


def call(kernel, out_shape, operands, in_specs=None, limit=16, scratch=(), flops=0, **kw):
    many = isinstance(out_shape, tuple)
    moved = sum(x.size * x.dtype.itemsize for x in operands)
    return pl.pallas_call(
        kernel,
        out_shape=out_shape,
        in_specs=in_specs or [VMEM] * len(operands),
        out_specs=kw.pop("out_specs", (VMEM,) * len(out_shape) if many else VMEM),
        scratch_shapes=list(scratch),
        compiler_params=pltpu.CompilerParams(vmem_limit_bytes=limit * MIB),
        cost_estimate=pl.CostEstimate(flops=flops, bytes_accessed=moved, transcendentals=0),
        **kw,
    )(*operands)


def load_each(refs, at, step):
    out = []
    for ref, n in refs:
        out += [ref[pl.ds(at * n + v, step, stride=n), :] for v in range(n)]
    return out


def pack_kernel(parts, blocks, x_ref, *o_refs):
    width = o_refs[0].shape[-1]

    @pl.loop(0, blocks, unroll=8)
    def _(b):
        x = x_ref[:, pl.ds(pl.multiple_of(b * width, width), width)]
        first = 0
        for ref, n in zip(o_refs, parts):
            ref[pl.ds(b * n, n), :] = x[first : first + n]
            first += n


def inner_kernel(parts, *refs):
    xs, (d_ref, o_ref) = list(zip(refs, parts)), refs[len(parts) :]
    vectors = sum(parts)
    blocks, width = d_ref.shape
    both = pairs(vectors)
    zero = jnp.zeros((8, width), F32)

    def step(c, sums):
        at = pl.multiple_of(c * 8, 8)
        d = d_ref[pl.ds(at, 8), :]
        x = load_each(xs, at, 8)
        y = [a * d for a in x]
        first = [s + x[i] * x[j] for s, (i, j) in zip(sums, both)]
        second = [s + x[i] * y[j] for s, (i, j) in zip(sums[len(both) :], both)]
        return tuple(first + second)

    sums = lax.fori_loop(0, blocks // 8, step, (zero,) * (2 * len(both)))
    for k, s in enumerate(sums):
        o_ref[pl.ds(8 * k, 8), :] = s


def pick_kernel(vectors, slots, where_ref, at_ref, *refs):
    pieces, outs = refs[:-2], refs[-2:]
    for which, out in enumerate(outs):

        @pl.loop(0, slots, unroll=4)
        def _(t):
            m = where_ref[which, t]
            at = at_ref[which, t]
            value = jnp.zeros((vectors, out.shape[-1]), F32)
            for k, piece in enumerate(pieces):
                value = jnp.where(m == k, piece[pl.ds(at, vectors), :], value)
            out[pl.ds(t * vectors, vectors), :] = value


def split(x):
    hi = x.astype(BF16)
    return hi, (x - hi.astype(F32)).astype(BF16)


def multiply_kernel(parts, step, transposed, x_refs, t_ref, o_ref):
    base = pl.program_id(0) * step
    width = o_ref.shape[-1]
    vectors = sum(parts)
    dims = (((1,), (1 if transposed else 0,)), ((), ()))

    def left(t):
        x = [ref[pl.ds(t * n, n), :] for ref, n in zip(x_refs, parts)]
        x = jnp.concatenate(x + [jnp.zeros((8 - vectors, width), F32)], axis=0)
        hi = x.astype(BF16).astype(F32)
        lo = x - hi
        top = jnp.concatenate([hi, hi], axis=1)
        low = jnp.concatenate([lo, jnp.zeros_like(lo)], axis=1)
        return [top, low]

    @pl.loop(0, step // 2)
    def _(p):
        i = 2 * p
        x = jnp.concatenate(left(base + i) + left(base + i + 1), axis=0).astype(BF16)
        along, across = (1, 0) if transposed else (0, 1)
        t = [jnp.concatenate(split(t_ref[i + k]), axis=along) for k in (0, 1)]
        y = lax.dot_general(x, jnp.concatenate(t, axis=across), dims, preferred_element_type=F32)
        o_ref[pl.ds((base + i) * vectors, vectors), :] = (y[0:8, :width] + y[8:16, :width])[:vectors]
        o_ref[pl.ds((base + i + 1) * vectors, vectors), :] = (y[16:24, width:] + y[24:32, width:])[:vectors]


def multiply(xs, tiles, ids, parts, transposed):
    slots, width, _ = tiles.shape
    step = max(s for s in (2, 4, 8, 16, 20) if slots % s == 0)
    rows = sum(parts) * slots
    spec = pl.BlockSpec((step, width, width), lambda i: (i, 0, 0))

    def kernel(*refs):
        x_refs, (t_ref, ids_ref, o_ref) = refs[: len(parts)], refs[len(parts) :]
        multiply_kernel(parts, step, transposed, x_refs, t_ref, o_ref)
        o_ref[pl.ds(rows, 8), :] = ids_ref[...]

    return call(
        kernel, jax.ShapeDtypeStruct((rows + 8, width), F32), (*xs, tiles, ids),
        [VMEM] * len(parts) + [spec, VMEM], 12, flops=slots * 2 * 32 * 256 * 128, grid=(slots // step,), out_specs=VMEM,
    )


def couple_kernel(parts, slots, *refs):
    xs, (y_ref, p_ref, o_ref) = list(zip(refs, parts)), refs[len(parts) :]
    vectors = sum(parts)
    both = pairs(vectors)
    n = len(both)

    def step(c, sums):
        at = pl.multiple_of(8 * c, 8)
        x = load_each(xs, at, 8)
        y = load_each([(y_ref, vectors)], at, 8)
        return tuple(s + (x[i] * y[j] + x[j] * y[i]) for s, (i, j) in zip(sums, both))

    sums = tuple(p_ref[pl.ds(8 * (n + k), 8), :] for k in range(n))
    sums = list(lax.fori_loop(0, slots // 8, step, sums))
    sums = [p_ref[pl.ds(8 * k, 8), :] for k in range(n)] + sums
    for k, s in enumerate(sums):
        o_ref[k : k + 1, :] = jnp.sum(s, axis=0, keepdims=True)
    if o_ref.shape[0] > 2 * n:
        o_ref[2 * n :, :] = jnp.zeros((o_ref.shape[0] - 2 * n, o_ref.shape[1]), F32)
    total = jnp.sum(o_ref[...], axis=1, keepdims=True)
    o_ref[...] = jnp.broadcast_to(total, o_ref.shape)


def add_kernel(vectors, slots, blocks, started, me_ref, *refs):
    o_ref, hot_ref = refs[-2:]
    lists = refs[:-2]
    if started:
        before, lists = lists[0], lists[1:]
    width = o_ref.shape[-1]
    row = lax.broadcasted_iota(jnp.int32, (blocks, width), 0) + me_ref[0] * blocks
    row = row.astype(F32)
    for k, ref in enumerate(lists):
        ids = ref[vectors * slots : vectors * slots + 1, :]
        hot_ref[:, k * width : (k + 1) * width] = jnp.where(ids == row, 1.0, 0.0).astype(BF16)
    group = 2 if vectors % 2 == 0 else 1
    pad = jnp.zeros((width - slots, group * width), F32)

    @pl.loop(0, vectors // group)
    def _(g):
        sums = None
        for k in range(0, len(lists), 2):
            parts = []
            for ref in lists[k : k + 2]:
                y = [ref[pl.ds(g * group + v, slots, stride=vectors), :] for v in range(group)]
                parts += [jnp.concatenate(y, axis=1), pad]
            y = jnp.concatenate(parts, axis=0)
            hi = y.astype(BF16)
            lo = (y - hi.astype(F32)).astype(BF16)
            hot = hot_ref[:, k * width : (k + 2) * width]
            part = jnp.dot(hot, hi, preferred_element_type=F32) + jnp.dot(hot, lo, preferred_element_type=F32)
            sums = part if sums is None else sums + part
        for v in range(group):
            at = pl.multiple_of((g * group + v) * blocks, 8)
            s = sums[:, v * width : (v + 1) * width]
            if started:
                s = s + before[pl.ds(at, blocks), :]
            o_ref[pl.ds(at, blocks), :] = s


def add_lists(me, lists, vectors, slots, blocks, before=None):
    width = lists[0].shape[-1]
    operands = (me,) + (() if before is None else (before,)) + tuple(lists)
    return call(
        functools.partial(add_kernel, vectors, slots, blocks, before is not None),
        jax.ShapeDtypeStruct((vectors * blocks, width), F32), operands,
        [SMEM] + [VMEM] * (len(operands) - 1), 16,
        scratch=(pltpu.VMEM((blocks, len(lists) * width), BF16),), flops=len(lists) * 2 * 256 * 256 * 768,
    )


def algebra(vectors, total, sums_ref):
    both = pairs(vectors)
    n = len(both)
    g, q = {}, {}
    for k, (i, j) in enumerate(both):
        g[i, j] = sums_ref[k : k + 1, :] * (1.0 / total)
        q[i, j] = q[j, i] = sums_ref[n + k : n + k + 1, :] * (1.0 / total)
    low, inv = {}, {}
    rev = []
    for j in range(vectors):
        s = g[j, j]
        for k in range(j):
            s = s - low[j, k] * low[j, k]
        rev.append(1.0 / jnp.sqrt(s))
        for i in range(j + 1, vectors):
            s = g[i, j]
            for k in range(j):
                s = s - low[i, k] * low[j, k]
            low[i, j] = s * rev[j]
    for j in range(vectors):
        inv[j, j] = rev[j]
        for i in range(j + 1, vectors):
            s = low[i, j] * inv[j, j]
            for k in range(j + 1, i):
                s = s + low[i, k] * inv[k, j]
            inv[i, j] = -s * rev[i]
    half, onto, proj = {}, {}, {}
    for i in range(vectors):
        for j in range(vectors):
            half[i, j] = sum(inv[i, k] * q[k, j] for k in range(i + 1))
    for i in range(vectors):
        for j in range(vectors):
            proj[i, j] = sum(half[i, k] * inv[j, k] for k in range(j + 1))
    for i in range(vectors):
        for j in range(vectors):
            onto[i, j] = sum(proj[i, k] * inv[k, j] for k in range(j, vectors))
    return inv, onto


def finish_kernel(parts, total, sums_ref, *refs):
    xs, (d_ref, m_ref, final_ref, residual_ref, coef, res, fin) = list(zip(refs, parts)), refs[len(parts) :]
    vectors = sum(parts)
    blocks, width = d_ref.shape
    inv, onto = algebra(vectors, total, sums_ref)
    places = {}
    for name, table in (("i", inv), ("o", onto)):
        for key in sorted(table):
            k = len(places)
            places[name, key] = k
            coef[pl.ds(8 * k, 8), :] = jnp.broadcast_to(table[key], (8, width))

    @pl.loop(0, blocks // 8, unroll=2)
    def _(c):
        at = pl.multiple_of(c * 8, 8)
        d = d_ref[pl.ds(at, 8), :]
        rd = 1.0 / d
        x = load_each(xs, at, 8)
        m = [m_ref[pl.ds(v * blocks + at, 8), :] + x[v] * d for v in range(vectors)]

        def value(name, i, j):
            return coef[pl.ds(8 * places[name, (i, j)], 8), :]

        for i in range(vectors):
            basis = r = None
            for j in range(i + 1):
                f = value("i", i, j)
                basis = f * x[j] if basis is None else basis + f * x[j]
                r = f * m[j] if r is None else r + f * m[j]
            for j in range(vectors):
                r = r - value("o", i, j) * x[j]
            res[pl.ds(8 * at + i, 8, stride=8), :] = r
            fin[pl.ds(8 * at + i, 8, stride=8), :] = basis - r * rd

    @pl.loop(0, blocks, unroll=8)
    def _(b):
        at = pl.multiple_of(b * width, width)
        residual_ref[:, pl.ds(at, width)] = res[pl.ds(pl.multiple_of(8 * b, 8), vectors), :]
        final_ref[:, pl.ds(at, width)] = fin[pl.ds(pl.multiple_of(8 * b, 8), vectors), :]


def body(start_block, diagonal, tile_values, tile_rows, tile_cols, tile_counts, offset_map):
    tiles = tile_values[0, 0]
    live_count = tile_counts[0, 0]
    row_size = lax.axis_size("row")
    off_size = lax.axis_size("off")
    me = lax.axis_index("off").astype(jnp.int32)
    vectors, shard = start_block.shape
    slots, width, _ = tiles.shape
    blocks = shard // width
    total = shard * off_size * row_size
    count = len(pairs(vectors))
    parts = [vectors - vectors // 2, vectors // 2]
    row_bits, off_bits = bits_of("row")[::-1], bits_of("off")

    packed = call(
        functools.partial(pack_kernel, parts, blocks),
        tuple(jax.ShapeDtypeStruct((n * blocks, width), F32) for n in parts), (start_block,),
    )
    live = jnp.arange(slots, dtype=jnp.int32) < live_count
    row_ids = jnp.where(live, tile_rows[0, 0], -1)
    col_ids = jnp.where(live, tile_cols[0, 0], -1)

    def padded(ids):
        return jnp.pad(ids.astype(F32)[None, :], ((0, 7), (0, width - slots)), constant_values=-1)

    diagonal = diagonal.reshape(blocks, width)

    arrangements = list(itertools.permutations(range(off_size))) if off_size <= 4 else []
    listed = off_size == row_size // 2 and arrangements
    if listed:
        matches = jnp.all(jnp.array(arrangements, jnp.int32) == offset_map[None, :], axis=1)
        which = jnp.argmax(matches).astype(jnp.int32)

    def routed(function, *operands):
        if listed:

            def branch(distances):
                return functools.partial(function, lambda x, sign: shift(x, [sign * d for d in distances]))

            return lax.switch(which, [branch(a) for a in arrangements], *operands)

        def move(x, sign):
            for b in range((row_size // 2).bit_length() - 1):
                moved = shift(x, [sign << b] * off_size)
                x = jnp.where(offset_map[me] >> b & 1 == 1, moved, x)
            return x

        return function(move, *operands)

    row_line, col_line = padded(row_ids), padded(col_ids)
    group_line = routed(lambda move, x: move(x, 1), col_line)
    both = jnp.stack([row_ids, group_line[0, :slots].astype(jnp.int32)])
    where = jnp.where(both < 0, -1, (both // blocks) ^ me)
    at = jnp.where(both < 0, 0, both % blocks)

    def pick(k, hold):
        n = parts[k]
        pieces = gather_off({0: packed[k]}, off_bits, hold)
        picked = jax.ShapeDtypeStruct((n * slots, width), F32)
        return call(
            functools.partial(pick_kernel, n, slots), (picked, picked),
            (where, at * n, *pieces), [SMEM, SMEM] + [VMEM] * off_size,
        )

    inner = call(
        functools.partial(inner_kernel, parts),
        jax.ShapeDtypeStruct((16 * count, width), F32), (*packed, diagonal),
    )
    row0, col0 = pick(0, (where, at, inner))
    arrived0 = routed(lambda move, x: move(x, -1), col0)
    row1, col1 = pick(1, (arrived0,))

    def run(move, rows, arrived0, col1, inner, tiles, row_line, col_line):
        arrived = [arrived0, move(col1, -1)]
        mirrored = multiply(rows, tiles, col_line, parts, False)
        returned = move(mirrored, 1)
        direct = multiply(arrived, tiles, row_line, parts, True)
        sums = call(
            functools.partial(couple_kernel, parts, slots),
            jax.ShapeDtypeStruct((-(-2 * count // 8) * 8, width), F32), (*rows, direct, inner),
        )
        stages = [sums]
        for axis, bit in [("off", off_bits[0])] + [("row", b) for b in row_bits[:-1]]:
            stages.append(sum_step(stages[-1], axis, bit))
        direct_over = swap(after(direct, stages[0]), "off", off_bits[0])
        returned_over = swap(after(returned, stages[1]), "off", off_bits[0])
        return stages[-1], direct, direct_over, returned, returned_over

    done = routed(run, [row0, row1], arrived0, col1, inner, tiles, row_line, col_line)
    sums, direct, direct_over, returned, returned_over = done
    top = off_bits[0]
    sums = sum_step(sums, "row", row_bits[-1])
    direct = gather_off({0: direct, top: direct_over}, off_bits[1:])
    returned = gather_off({0: returned, top: returned_over}, off_bits[1:])
    lists = [y for pair in zip(direct, returned) for y in pair]
    image = add_lists(me[None], lists[:off_size], vectors, slots, blocks)
    image = add_lists(me[None], lists[off_size:], vectors, slots, blocks, image)
    sums = after(sums, image)
    for bit in off_bits[1:]:
        sums = sum_step(sums, "off", bit)
    out = jax.ShapeDtypeStruct((vectors, shard), F32)
    return call(
        functools.partial(finish_kernel, parts, float(total)), (out, out),
        (sums, *packed, diagonal, image), limit=24,
        scratch=(
            pltpu.VMEM((8 * (vectors * vectors + count), width), F32),
            pltpu.VMEM((8 * blocks, width), F32),
            pltpu.VMEM((8 * blocks, width), F32),
        ),
    )


def solution(mesh):
    return jax.shard_map(
        body,
        mesh=mesh,
        in_specs=(
            P(None, ("row", "off")),
            P(("row", "off")),
            P("row", "off", None, None, None),
            P("row", "off", None),
            P("row", "off", None),
            P("row", "off"),
            P(),
        ),
        out_specs=(P(None, ("row", "off")), P(None, ("row", "off"))),
        check_vma=False,
    )
```

```python
import functools

import jax
import jax.numpy as jnp
from jax import lax
from jax.experimental import pallas as pl
from jax.experimental.pallas import tpu as pltpu
from jax.sharding import PartitionSpec as P


VMEM = pl.BlockSpec(memory_space=pltpu.VMEM)
SMEM = pl.BlockSpec(memory_space=pltpu.SMEM)
MIB = 1 << 20
BF16 = jnp.bfloat16
F32 = jnp.float32


def swap(x, axis, mask):
    n = lax.axis_size(axis)
    return lax.ppermute(x, axis, [(i, i ^ mask) for i in range(n)])


def shift(x, distance):
    n = lax.axis_size("row")
    if distance == 0:
        return x
    return lax.ppermute(x, "row", [(i, (i + distance) % n) for i in range(n)])


def after(x, *others):
    return lax.optimization_barrier((x, *others))[0]


def bits_of(axis):
    return [1 << b for b in reversed(range(lax.axis_size(axis).bit_length() - 1))]


def gather_off(pieces, bits, hold=()):
    pieces = dict(pieces)
    for bit in bits:
        for m in list(pieces):
            source = after(pieces[m], *hold) if m and hold else pieces[m]
            pieces[m | bit] = swap(source, "off", bit)
    return [pieces[m] for m in sorted(pieces)]


def sum_step(x, axis, bit):
    return x + swap(x, axis, bit)


def pairs(vectors):
    return [(i, j) for i in range(vectors) for j in range(i + 1)]


def call(kernel, out_shape, operands, in_specs=None, limit=16, scratch=(), flops=0, **kw):
    many = isinstance(out_shape, tuple)
    moved = sum(x.size * x.dtype.itemsize for x in operands)
    return pl.pallas_call(
        kernel,
        out_shape=out_shape,
        in_specs=in_specs or [VMEM] * len(operands),
        out_specs=kw.pop("out_specs", (VMEM,) * len(out_shape) if many else VMEM),
        scratch_shapes=list(scratch),
        compiler_params=pltpu.CompilerParams(vmem_limit_bytes=limit * MIB),
        cost_estimate=pl.CostEstimate(flops=flops, bytes_accessed=moved, transcendentals=0),
        **kw,
    )(*operands)


def load_each(refs, at, step):
    out = []
    for ref, n in refs:
        out += [ref[pl.ds(at * n + v, step, stride=n), :] for v in range(n)]
    return out


def pack_kernel(parts, blocks, x_ref, *o_refs):
    width = o_refs[0].shape[-1]

    @pl.loop(0, blocks, unroll=8)
    def _(b):
        x = x_ref[:, pl.ds(pl.multiple_of(b * width, width), width)]
        first = 0
        for ref, n in zip(o_refs, parts):
            ref[pl.ds(b * n, n), :] = x[first : first + n]
            first += n


def inner_kernel(parts, *refs):
    xs, (d_ref, o_ref) = list(zip(refs, parts)), refs[len(parts) :]
    vectors = sum(parts)
    blocks, width = d_ref.shape
    both = pairs(vectors)
    zero = jnp.zeros((8, width), F32)

    def step(c, sums):
        at = pl.multiple_of(c * 8, 8)
        d = d_ref[pl.ds(at, 8), :]
        x = load_each(xs, at, 8)
        y = [a * d for a in x]
        first = [s + x[i] * x[j] for s, (i, j) in zip(sums, both)]
        second = [s + x[i] * y[j] for s, (i, j) in zip(sums[len(both) :], both)]
        return tuple(first + second)

    sums = lax.fori_loop(0, blocks // 8, step, (zero,) * (2 * len(both)))
    for k, s in enumerate(sums):
        o_ref[pl.ds(8 * k, 8), :] = s


def divide_kernel(t_ref, hi_ref, lo_ref):
    t = t_ref[...]
    hi = t.astype(BF16)
    hi_ref[...] = hi
    lo_ref[...] = (t - hi.astype(F32)).astype(BF16)


def divide(tiles):
    slots, width, _ = tiles.shape
    step = max(s for s in (1, 2, 4, 8) if slots % s == 0)
    spec = pl.BlockSpec((step, width, width), lambda i: (i, 0, 0))
    shape = jax.ShapeDtypeStruct(tiles.shape, BF16)
    return call(
        divide_kernel, (shape, shape), (tiles,), [spec], 8,
        flops=tiles.size * 4, grid=(slots // step,), out_specs=(spec, spec),
    )


def pick_kernel(vectors, slots, where_ref, at_ref, *refs):
    pieces, outs = refs[:-2], refs[-2:]
    for which, out in enumerate(outs):

        @pl.loop(0, slots, unroll=4)
        def _(t):
            m = where_ref[which, t]
            at = at_ref[which, t]
            value = jnp.zeros((vectors, out.shape[-1]), F32)
            for k, piece in enumerate(pieces):
                value = jnp.where(m == k, piece[pl.ds(at, vectors), :], value)
            out[pl.ds(t * vectors, vectors), :] = value


def multiply_kernel(parts, outs, step, transposed, x_refs, hi_ref, lo_ref, o_refs):
    base = pl.program_id(0) * step
    width = hi_ref.shape[-1]
    vectors = sum(parts)
    dims = (((1,), (1 if transposed else 0,)), ((), ()))

    def left(t):
        x = [ref[pl.ds(t * n, n), :] for ref, n in zip(x_refs, parts)]
        x = jnp.concatenate(x + [jnp.zeros((8 - vectors, width), F32)], axis=0)
        hi = x.astype(BF16).astype(F32)
        lo = x - hi
        top = jnp.concatenate([hi, hi], axis=1)
        low = jnp.concatenate([lo, jnp.zeros_like(lo)], axis=1)
        return [top, low]

    def put(t, y):
        first = 0
        for ref, n in zip(o_refs, outs):
            ref[pl.ds(t * n, n), :] = y[first : first + n]
            first += n

    @pl.loop(0, step // 2, unroll=2)
    def _(p):
        i = 2 * p
        x = jnp.concatenate(left(base + i) + left(base + i + 1), axis=0).astype(BF16)
        along, across = (1, 0) if transposed else (0, 1)
        t = [jnp.concatenate([hi_ref[i + k], lo_ref[i + k]], axis=along) for k in (0, 1)]
        y = lax.dot_general(x, jnp.concatenate(t, axis=across), dims, preferred_element_type=F32)
        put(base + i, y[0:8, :width] + y[8:16, :width])
        put(base + i + 1, y[16:24, width:] + y[24:32, width:])


def multiply(xs, high, low, ids, parts, outs, transposed):
    slots, width, _ = high.shape
    step = max(s for s in (2, 4, 8, 16, 20) if slots % s == 0)
    spec = pl.BlockSpec((step, width, width), lambda i: (i, 0, 0))

    def kernel(*refs):
        x_refs, (hi_ref, lo_ref, ids_ref), o_refs = refs[: len(parts)], refs[len(parts) :][:3], refs[len(parts) + 3 :]
        multiply_kernel(parts, outs, step, transposed, x_refs, hi_ref, lo_ref, o_refs)
        for ref, n in zip(o_refs, outs):
            ref[pl.ds(n * slots, 8), :] = ids_ref[...]

    return call(
        kernel, tuple(jax.ShapeDtypeStruct((n * slots + 8, width), F32) for n in outs),
        (*xs, high, low, ids), [VMEM] * len(parts) + [spec, spec, VMEM], 12,
        flops=slots * 2 * 32 * 256 * 128, grid=(slots // step,),
    )


def couple_kernel(parts, slots, *refs):
    xs, (y_ref, p_ref, o_ref) = list(zip(refs, parts)), refs[len(parts) :]
    vectors = sum(parts)
    both = pairs(vectors)
    n = len(both)

    def step(c, sums):
        at = pl.multiple_of(8 * c, 8)
        x = load_each(xs, at, 8)
        y = load_each([(y_ref, vectors)], at, 8)
        return tuple(s + (x[i] * y[j] + x[j] * y[i]) for s, (i, j) in zip(sums, both))

    sums = tuple(p_ref[pl.ds(8 * (n + k), 8), :] for k in range(n))
    sums = list(lax.fori_loop(0, slots // 8, step, sums))
    sums = [p_ref[pl.ds(8 * k, 8), :] for k in range(n)] + sums
    for k, s in enumerate(sums):
        o_ref[k : k + 1, :] = jnp.sum(s, axis=0, keepdims=True)
    if o_ref.shape[0] > 2 * n:
        o_ref[2 * n :, :] = jnp.zeros((o_ref.shape[0] - 2 * n, o_ref.shape[1]), F32)
    total = jnp.sum(o_ref[...], axis=1, keepdims=True)
    o_ref[...] = jnp.broadcast_to(total, o_ref.shape)


def add_kernel(shapes, slots, blocks, started, me_ref, *refs):
    o_ref, refs = refs[-1], list(refs[:-1])
    before = refs.pop(0) if started else None
    lists = [[(refs.pop(0), n) for n in shape] for shape in shapes]
    vectors = sum(shapes[0])
    width = o_ref.shape[-1]
    row = lax.broadcasted_iota(jnp.int32, (blocks, width), 0) + me_ref[0] * blocks
    row = row.astype(F32)
    pad = jnp.zeros((width - slots, vectors * width), F32)
    sums = None
    for k in range(0, len(lists), 2):
        hots, blocks_of = [], []
        for parts in lists[k : k + 2]:
            ref, n = parts[0]
            ids = ref[n * slots : n * slots + 1, :]
            hots.append(jnp.where(ids == row, 1.0, 0.0).astype(BF16))
            blocks_of += [jnp.concatenate(load_each(parts, 0, slots), axis=1), pad]
        hot = jnp.concatenate(hots, axis=1)
        y = jnp.concatenate(blocks_of, axis=0)
        hi = y.astype(BF16)
        lo = (y - hi.astype(F32)).astype(BF16)
        part = jnp.dot(hot, hi, preferred_element_type=F32) + jnp.dot(hot, lo, preferred_element_type=F32)
        sums = part if sums is None else sums + part
    for v in range(vectors):
        s = sums[:, v * width : (v + 1) * width]
        if started:
            s = s + before[pl.ds(v * blocks, blocks), :]
        o_ref[pl.ds(v * blocks, blocks), :] = s


def add_lists(me, lists, slots, blocks, before=None):
    width = lists[0][0].shape[-1]
    shapes = [tuple(x.shape[0] // slots for x in parts) for parts in lists]
    operands = (me,) + (() if before is None else (before,)) + tuple(x for parts in lists for x in parts)
    return call(
        functools.partial(add_kernel, shapes, slots, blocks, before is not None),
        jax.ShapeDtypeStruct((sum(shapes[0]) * blocks, width), F32), operands,
        [SMEM] + [VMEM] * (len(operands) - 1), 16, flops=len(lists) * 2 * 256 * 256 * 768,
    )


def algebra(vectors, total, sums_ref):
    both = pairs(vectors)
    n = len(both)
    g, q = {}, {}
    for k, (i, j) in enumerate(both):
        g[i, j] = sums_ref[k : k + 1, :] * (1.0 / total)
        q[i, j] = q[j, i] = sums_ref[n + k : n + k + 1, :] * (1.0 / total)
    low, inv = {}, {}
    rev = []
    for j in range(vectors):
        s = g[j, j]
        for k in range(j):
            s = s - low[j, k] * low[j, k]
        rev.append(1.0 / jnp.sqrt(s))
        for i in range(j + 1, vectors):
            s = g[i, j]
            for k in range(j):
                s = s - low[i, k] * low[j, k]
            low[i, j] = s * rev[j]
    for j in range(vectors):
        inv[j, j] = rev[j]
        for i in range(j + 1, vectors):
            s = low[i, j] * inv[j, j]
            for k in range(j + 1, i):
                s = s + low[i, k] * inv[k, j]
            inv[i, j] = -s * rev[i]
    half, onto, proj = {}, {}, {}
    for i in range(vectors):
        for j in range(vectors):
            half[i, j] = sum(inv[i, k] * q[k, j] for k in range(i + 1))
    for i in range(vectors):
        for j in range(vectors):
            proj[i, j] = sum(half[i, k] * inv[j, k] for k in range(j + 1))
    for i in range(vectors):
        for j in range(vectors):
            onto[i, j] = sum(proj[i, k] * inv[k, j] for k in range(j, vectors))
    return inv, onto


def finish_kernel(parts, total, sums_ref, *refs):
    xs, (d_ref, m_ref, final_ref, residual_ref, coef, res, fin) = list(zip(refs, parts)), refs[len(parts) :]
    vectors = sum(parts)
    blocks, width = d_ref.shape
    inv, onto = algebra(vectors, total, sums_ref)
    places = {}
    for name, table in (("i", inv), ("o", onto)):
        for key in sorted(table):
            k = len(places)
            places[name, key] = k
            coef[pl.ds(8 * k, 8), :] = jnp.broadcast_to(table[key], (8, width))

    @pl.loop(0, blocks // 8, unroll=2)
    def _(c):
        at = pl.multiple_of(c * 8, 8)
        d = d_ref[pl.ds(at, 8), :]
        rd = 1.0 / d
        x = load_each(xs, at, 8)
        m = [m_ref[pl.ds(v * blocks + at, 8), :] + x[v] * d for v in range(vectors)]

        def value(name, i, j):
            return coef[pl.ds(8 * places[name, (i, j)], 8), :]

        for i in range(vectors):
            basis = r = None
            for j in range(i + 1):
                f = value("i", i, j)
                basis = f * x[j] if basis is None else basis + f * x[j]
                r = f * m[j] if r is None else r + f * m[j]
            for j in range(vectors):
                r = r - value("o", i, j) * x[j]
            res[pl.ds(8 * at + i, 8, stride=8), :] = r
            fin[pl.ds(8 * at + i, 8, stride=8), :] = basis - r * rd

    @pl.loop(0, blocks, unroll=8)
    def _(b):
        at = pl.multiple_of(b * width, width)
        residual_ref[:, pl.ds(at, width)] = res[pl.ds(pl.multiple_of(8 * b, 8), vectors), :]
        final_ref[:, pl.ds(at, width)] = fin[pl.ds(pl.multiple_of(8 * b, 8), vectors), :]


def body(start_block, diagonal, tile_values, tile_rows, tile_cols, tile_counts, offset_map):
    tiles = tile_values[0, 0]
    live_count = tile_counts[0, 0]
    row_size = lax.axis_size("row")
    off_size = lax.axis_size("off")
    me = lax.axis_index("off").astype(jnp.int32)
    vectors, shard = start_block.shape
    slots, width, _ = tiles.shape
    blocks = shard // width
    total = shard * off_size * row_size
    count = len(pairs(vectors))
    parts = [vectors - vectors // 2, vectors // 2]
    row_bits, off_bits = bits_of("row")[::-1], bits_of("off")

    packed = call(
        functools.partial(pack_kernel, parts, blocks),
        tuple(jax.ShapeDtypeStruct((n * blocks, width), F32) for n in parts), (start_block,),
    )
    live = jnp.arange(slots, dtype=jnp.int32) < live_count
    row_ids = jnp.where(live, tile_rows[0, 0], -1)
    col_ids = jnp.where(live, tile_cols[0, 0], -1)

    def padded(ids):
        return jnp.pad(ids.astype(F32)[None, :], ((0, 7), (0, width - slots)), constant_values=-1)

    diagonal = diagonal.reshape(blocks, width)

    offset = offset_map[me]
    steps = row_size // 2

    def routed(function, *operands):
        if steps <= 4:

            def branch(s):
                return functools.partial(function, lambda x, sign: shift(x, sign * s))

            return lax.switch(offset, [branch(s) for s in range(steps)], *operands)

        def move(x, sign):
            for b in range(steps.bit_length() - 1):
                x = jnp.where(offset >> b & 1 == 1, shift(x, sign << b), x)
            return x

        return function(move, *operands)

    row_line, col_line = padded(row_ids), padded(col_ids)
    group_line = routed(lambda move, x: move(x, 1), col_line)
    both = jnp.stack([row_ids, group_line[0, :slots].astype(jnp.int32)])
    where = jnp.where(both < 0, -1, (both // blocks) ^ me)
    at = jnp.where(both < 0, 0, both % blocks)

    def pick(k, hold):
        n = parts[k]
        pieces = gather_off({0: packed[k]}, off_bits, hold)
        picked = jax.ShapeDtypeStruct((n * slots, width), F32)
        return call(
            functools.partial(pick_kernel, n, slots), (picked, picked),
            (where, at * n, *pieces), [SMEM, SMEM] + [VMEM] * off_size,
        )

    row0, col0 = pick(0, (where, at))

    def first(move, col, packed, diagonal, tiles):
        arrived = move(col, -1)
        inner = call(
            functools.partial(inner_kernel, parts),
            jax.ShapeDtypeStruct((16 * count, width), F32), (*packed, diagonal),
        )
        high, low = divide(tiles)
        return arrived, inner, high, low

    arrived0, inner, high, low = routed(first, col0, packed, diagonal, tiles)
    row1, col1 = pick(1, (arrived0,))

    def second(move, rows, arrived0, col1, high, low, row_line, col_line):
        arrived = [arrived0, move(col1, -1)]
        mirrored, later = multiply(rows, high, low, col_line, parts, parts, False)
        returned = move(mirrored, 1)
        (direct,) = multiply(arrived, high, low, row_line, parts, [vectors], True)
        return direct, returned, later

    rows = [row0, row1]
    direct, returned, later = routed(second, rows, arrived0, col1, high, low, row_line, col_line)
    sums = call(
        functools.partial(couple_kernel, parts, slots),
        jax.ShapeDtypeStruct((-(-2 * count // 8) * 8, width), F32), (*rows, direct, inner),
    )
    top = off_bits[0]
    partial_sums = sums
    sums = sum_step(sums, "off", top)
    direct_over = swap(after(direct, partial_sums), "off", top)
    returned_over = swap(after(returned, partial_sums), "off", top)

    def third(move, later, sums):
        returned = move(later, 1)
        for bit in row_bits[:-1]:
            sums = sum_step(sums, "row", bit)
        return returned, sums

    later, sums = routed(third, later, sums)
    later_over = swap(later, "off", top)
    sums = sum_step(sums, "row", row_bits[-1])
    direct = gather_off({0: direct, top: direct_over}, off_bits[1:])
    returned = gather_off({0: returned, top: returned_over}, off_bits[1:])
    later = gather_off({0: later, top: later_over}, off_bits[1:])
    lists = []
    for a, b, c in zip(direct, returned, later):
        lists += [(a,), (b, c)]
    image = add_lists(me[None], lists[:off_size], slots, blocks)
    sums = after(sums, image)
    for bit in off_bits[1:]:
        sums = sum_step(sums, "off", bit)
    image = add_lists(me[None], lists[off_size:], slots, blocks, image)
    out = jax.ShapeDtypeStruct((vectors, shard), F32)
    return call(
        functools.partial(finish_kernel, parts, float(total)), (out, out),
        (sums, *packed, diagonal, image), limit=24,
        scratch=(
            pltpu.VMEM((8 * (vectors * vectors + count), width), F32),
            pltpu.VMEM((8 * blocks, width), F32),
            pltpu.VMEM((8 * blocks, width), F32),
        ),
    )


def solution(mesh):
    return jax.shard_map(
        body,
        mesh=mesh,
        in_specs=(
            P(None, ("row", "off")),
            P(("row", "off")),
            P("row", "off", None, None, None),
            P("row", "off", None),
            P("row", "off", None),
            P("row", "off"),
            P(),
        ),
        out_specs=(P(None, ("row", "off")), P(None, ("row", "off"))),
        check_vma=False,
    )
```

```python
import functools

import jax
import jax.numpy as jnp
from jax import lax
from jax.experimental import pallas as pl
from jax.experimental.pallas import tpu as pltpu
from jax.sharding import PartitionSpec as P


VMEM = pl.BlockSpec(memory_space=pltpu.VMEM)
SMEM = pl.BlockSpec(memory_space=pltpu.SMEM)
MIB = 1 << 20
BF16 = jnp.bfloat16
F32 = jnp.float32


def swap(x, axis, mask):
    n = lax.axis_size(axis)
    return lax.ppermute(x, axis, [(i, i ^ mask) for i in range(n)])


def shift(x, distance):
    n = lax.axis_size("row")
    if distance == 0:
        return x
    return lax.ppermute(x, "row", [(i, (i + distance) % n) for i in range(n)])


def after(x, *others):
    return lax.optimization_barrier((x, *others))[0]


def bits_of(axis):
    return [1 << b for b in reversed(range(lax.axis_size(axis).bit_length() - 1))]


def gather_off(pieces, bits, hold=()):
    pieces = dict(pieces)
    for bit in bits:
        for m in list(pieces):
            source = after(pieces[m], *hold) if m and hold else pieces[m]
            pieces[m | bit] = swap(source, "off", bit)
    return [pieces[m] for m in sorted(pieces)]


def sum_step(x, axis, bit):
    return x + swap(x, axis, bit)


def pairs(vectors):
    return [(i, j) for i in range(vectors) for j in range(i + 1)]


def call(kernel, out_shape, operands, in_specs=None, limit=16, scratch=(), flops=0, **kw):
    many = isinstance(out_shape, tuple)
    moved = sum(x.size * x.dtype.itemsize for x in operands)
    return pl.pallas_call(
        kernel,
        out_shape=out_shape,
        in_specs=in_specs or [VMEM] * len(operands),
        out_specs=kw.pop("out_specs", (VMEM,) * len(out_shape) if many else VMEM),
        scratch_shapes=list(scratch),
        compiler_params=pltpu.CompilerParams(vmem_limit_bytes=limit * MIB),
        cost_estimate=pl.CostEstimate(flops=flops, bytes_accessed=moved, transcendentals=0),
        **kw,
    )(*operands)


def load_each(refs, at, step):
    out = []
    for ref, n in refs:
        out += [ref[pl.ds(at * n + v, step, stride=n), :] for v in range(n)]
    return out


def pack_kernel(parts, blocks, x_ref, *o_refs):
    width = o_refs[0].shape[-1]

    @pl.loop(0, blocks, unroll=8)
    def _(b):
        x = x_ref[:, pl.ds(pl.multiple_of(b * width, width), width)]
        first = 0
        for ref, n in zip(o_refs, parts):
            ref[pl.ds(b * n, n), :] = x[first : first + n]
            first += n


def prepare_kernel(parts, slots, me_ref, count_ref, map_ref, rows_ref, cols_ref, *refs):
    xs, (d_ref, ids_ref, offset_ref, o_ref) = list(zip(refs, parts)), refs[len(parts) :]
    offset_ref[0] = map_ref[me_ref[0]]
    live = lax.broadcasted_iota(jnp.int32, (1, slots), 1) < count_ref[0, 0]
    ids_ref[...] = jnp.full(ids_ref.shape, -1, jnp.int32)
    ids_ref[0:1, :slots] = jnp.where(live, rows_ref[...], -1)
    ids_ref[1:2, :slots] = jnp.where(live, cols_ref[...], -1)
    vectors = sum(parts)
    blocks, width = d_ref.shape
    both = pairs(vectors)
    zero = jnp.zeros((8, width), F32)

    def step(c, sums):
        at = pl.multiple_of(c * 8, 8)
        d = d_ref[pl.ds(at, 8), :]
        x = load_each(xs, at, 8)
        y = [a * d for a in x]
        first = [s + x[i] * x[j] for s, (i, j) in zip(sums, both)]
        second = [s + x[i] * y[j] for s, (i, j) in zip(sums[len(both) :], both)]
        return tuple(first + second)

    sums = lax.fori_loop(0, blocks // 8, step, (zero,) * (2 * len(both)))
    for k, s in enumerate(sums):
        o_ref[pl.ds(8 * k, 8), :] = s


def divide_kernel(t_ref, hi_ref, lo_ref):
    t = t_ref[...]
    hi = t.astype(BF16)
    hi_ref[...] = hi
    lo_ref[...] = (t - hi.astype(F32)).astype(BF16)


def divide(tiles):
    slots, width, _ = tiles.shape
    step = max(s for s in (1, 2, 4, 8) if slots % s == 0)
    spec = pl.BlockSpec((step, width, width), lambda i: (i, 0, 0))
    shape = jax.ShapeDtypeStruct(tiles.shape, BF16)
    return call(
        divide_kernel, (shape, shape), (tiles,), [spec], 8,
        flops=tiles.size * 4, grid=(slots // step,), out_specs=(spec, spec),
    )


def pick_kernel(vectors, slots, blocks, me_ref, own_ref, other_ref, *refs):
    pieces, outs = refs[:-2], refs[-2:]
    me = me_ref[0]
    for ids_ref, line, out in ((own_ref, 0, outs[0]), (other_ref, 1, outs[1])):

        @pl.loop(0, slots, unroll=4)
        def _(t):
            b = ids_ref[line, t]
            place = jnp.maximum(b, 0)
            m = jnp.where(b < 0, -1, (place // blocks) ^ me)
            at = (place % blocks) * vectors
            value = jnp.zeros((vectors, out.shape[-1]), F32)
            for k, piece in enumerate(pieces):
                value = jnp.where(m == k, piece[pl.ds(at, vectors), :], value)
            out[pl.ds(t * vectors, vectors), :] = value


def multiply_kernel(parts, outs, step, transposed, x_refs, hi_ref, lo_ref, o_refs):
    base = pl.program_id(0) * step
    width = hi_ref.shape[-1]
    vectors = sum(parts)
    dims = (((1,), (1 if transposed else 0,)), ((), ()))

    def left(t):
        x = [ref[pl.ds(t * n, n), :] for ref, n in zip(x_refs, parts)]
        x = jnp.concatenate(x + [jnp.zeros((8 - vectors, width), F32)], axis=0)
        hi = x.astype(BF16).astype(F32)
        lo = x - hi
        top = jnp.concatenate([hi, hi], axis=1)
        low = jnp.concatenate([lo, jnp.zeros_like(lo)], axis=1)
        return [top, low]

    def put(t, y):
        first = 0
        for ref, n in zip(o_refs, outs):
            ref[pl.ds(t * n, n), :] = y[first : first + n]
            first += n

    @pl.loop(0, step // 2, unroll=2)
    def _(p):
        i = 2 * p
        x = jnp.concatenate(left(base + i) + left(base + i + 1), axis=0).astype(BF16)
        along, across = (1, 0) if transposed else (0, 1)
        t = [jnp.concatenate([hi_ref[i + k], lo_ref[i + k]], axis=along) for k in (0, 1)]
        y = lax.dot_general(x, jnp.concatenate(t, axis=across), dims, preferred_element_type=F32)
        put(base + i, y[0:8, :width] + y[8:16, :width])
        put(base + i + 1, y[16:24, width:] + y[24:32, width:])


def multiply(xs, high, low, ids, line, parts, outs, transposed):
    slots, width, _ = high.shape
    step = max(s for s in (2, 4, 8, 16, 20) if slots % s == 0)
    spec = pl.BlockSpec((step, width, width), lambda i: (i, 0, 0))

    def kernel(*refs):
        x_refs, (hi_ref, lo_ref, ids_ref), o_refs = refs[: len(parts)], refs[len(parts) :][:3], refs[len(parts) + 3 :]
        multiply_kernel(parts, outs, step, transposed, x_refs, hi_ref, lo_ref, o_refs)
        for ref, n in zip(o_refs, outs):
            ref[pl.ds(n * slots, 8), :] = jnp.broadcast_to(ids_ref[line : line + 1, :], (8, width)).astype(F32)

    return call(
        kernel, tuple(jax.ShapeDtypeStruct((n * slots + 8, width), F32) for n in outs),
        (*xs, high, low, ids), [VMEM] * len(parts) + [spec, spec, VMEM], 12,
        flops=slots * 2 * 32 * 256 * 128, grid=(slots // step,),
    )


def couple_kernel(parts, slots, *refs):
    xs, (y_ref, p_ref, o_ref) = list(zip(refs, parts)), refs[len(parts) :]
    vectors = sum(parts)
    both = pairs(vectors)
    n = len(both)

    def step(c, sums):
        at = pl.multiple_of(8 * c, 8)
        x = load_each(xs, at, 8)
        y = load_each([(y_ref, vectors)], at, 8)
        return tuple(s + (x[i] * y[j] + x[j] * y[i]) for s, (i, j) in zip(sums, both))

    sums = tuple(p_ref[pl.ds(8 * (n + k), 8), :] for k in range(n))
    sums = list(lax.fori_loop(0, slots // 8, step, sums))
    sums = [p_ref[pl.ds(8 * k, 8), :] for k in range(n)] + sums
    for k, s in enumerate(sums):
        o_ref[k : k + 1, :] = jnp.sum(s, axis=0, keepdims=True)
    if o_ref.shape[0] > 2 * n:
        o_ref[2 * n :, :] = jnp.zeros((o_ref.shape[0] - 2 * n, o_ref.shape[1]), F32)
    total = jnp.sum(o_ref[...], axis=1, keepdims=True)
    o_ref[...] = jnp.broadcast_to(total, o_ref.shape)


def add_kernel(shapes, slots, blocks, started, me_ref, *refs):
    o_ref, refs = refs[-1], list(refs[:-1])
    before = refs.pop(0) if started else None
    lists = [[(refs.pop(0), n) for n in shape] for shape in shapes]
    vectors = sum(shapes[0])
    width = o_ref.shape[-1]
    row = lax.broadcasted_iota(jnp.int32, (blocks, width), 0) + me_ref[0] * blocks
    row = row.astype(F32)
    pad = jnp.zeros((width - slots, vectors * width), F32)
    sums = None
    for k in range(0, len(lists), 2):
        hots, blocks_of = [], []
        for parts in lists[k : k + 2]:
            ref, n = parts[0]
            ids = ref[n * slots : n * slots + 1, :]
            hots.append(jnp.where(ids == row, 1.0, 0.0).astype(BF16))
            blocks_of += [jnp.concatenate(load_each(parts, 0, slots), axis=1), pad]
        hot = jnp.concatenate(hots, axis=1)
        y = jnp.concatenate(blocks_of, axis=0)
        hi = y.astype(BF16)
        lo = (y - hi.astype(F32)).astype(BF16)
        part = jnp.dot(hot, hi, preferred_element_type=F32) + jnp.dot(hot, lo, preferred_element_type=F32)
        sums = part if sums is None else sums + part
    for v in range(vectors):
        s = sums[:, v * width : (v + 1) * width]
        if started:
            s = s + before[pl.ds(v * blocks, blocks), :]
        o_ref[pl.ds(v * blocks, blocks), :] = s


def add_lists(me, lists, slots, blocks, before=None):
    width = lists[0][0].shape[-1]
    shapes = [tuple(x.shape[0] // slots for x in parts) for parts in lists]
    operands = (me,) + (() if before is None else (before,)) + tuple(x for parts in lists for x in parts)
    return call(
        functools.partial(add_kernel, shapes, slots, blocks, before is not None),
        jax.ShapeDtypeStruct((sum(shapes[0]) * blocks, width), F32), operands,
        [SMEM] + [VMEM] * (len(operands) - 1), 16, flops=len(lists) * 2 * 256 * 256 * 768,
    )


def algebra(vectors, total, sums_ref):
    both = pairs(vectors)
    n = len(both)
    g, q = {}, {}
    for k, (i, j) in enumerate(both):
        g[i, j] = sums_ref[k : k + 1, :] * (1.0 / total)
        q[i, j] = q[j, i] = sums_ref[n + k : n + k + 1, :] * (1.0 / total)
    low, inv = {}, {}
    rev = []
    for j in range(vectors):
        s = g[j, j]
        for k in range(j):
            s = s - low[j, k] * low[j, k]
        rev.append(1.0 / jnp.sqrt(s))
        for i in range(j + 1, vectors):
            s = g[i, j]
            for k in range(j):
                s = s - low[i, k] * low[j, k]
            low[i, j] = s * rev[j]
    for j in range(vectors):
        inv[j, j] = rev[j]
        for i in range(j + 1, vectors):
            s = low[i, j] * inv[j, j]
            for k in range(j + 1, i):
                s = s + low[i, k] * inv[k, j]
            inv[i, j] = -s * rev[i]
    half, onto, proj = {}, {}, {}
    for i in range(vectors):
        for j in range(vectors):
            half[i, j] = sum(inv[i, k] * q[k, j] for k in range(i + 1))
    for i in range(vectors):
        for j in range(vectors):
            proj[i, j] = sum(half[i, k] * inv[j, k] for k in range(j + 1))
    for i in range(vectors):
        for j in range(vectors):
            onto[i, j] = sum(proj[i, k] * inv[k, j] for k in range(j, vectors))
    return inv, onto


def finish_kernel(parts, total, sums_ref, *refs):
    xs, (d_ref, m_ref, final_ref, residual_ref, coef, res, fin) = list(zip(refs, parts)), refs[len(parts) :]
    vectors = sum(parts)
    blocks, width = d_ref.shape
    inv, onto = algebra(vectors, total, sums_ref)
    places = {}
    for name, table in (("i", inv), ("o", onto)):
        for key in sorted(table):
            k = len(places)
            places[name, key] = k
            coef[pl.ds(8 * k, 8), :] = jnp.broadcast_to(table[key], (8, width))

    @pl.loop(0, blocks // 8, unroll=2)
    def _(c):
        at = pl.multiple_of(c * 8, 8)
        d = d_ref[pl.ds(at, 8), :]
        rd = 1.0 / d
        x = load_each(xs, at, 8)
        m = [m_ref[pl.ds(v * blocks + at, 8), :] + x[v] * d for v in range(vectors)]

        def value(name, i, j):
            return coef[pl.ds(8 * places[name, (i, j)], 8), :]

        for i in range(vectors):
            basis = r = None
            for j in range(i + 1):
                f = value("i", i, j)
                basis = f * x[j] if basis is None else basis + f * x[j]
                r = f * m[j] if r is None else r + f * m[j]
            for j in range(vectors):
                r = r - value("o", i, j) * x[j]
            res[pl.ds(8 * at + i, 8, stride=8), :] = r
            fin[pl.ds(8 * at + i, 8, stride=8), :] = basis - r * rd

    @pl.loop(0, blocks, unroll=8)
    def _(b):
        at = pl.multiple_of(b * width, width)
        residual_ref[:, pl.ds(at, width)] = res[pl.ds(pl.multiple_of(8 * b, 8), vectors), :]
        final_ref[:, pl.ds(at, width)] = fin[pl.ds(pl.multiple_of(8 * b, 8), vectors), :]


def body(start_block, diagonal, tile_values, tile_rows, tile_cols, tile_counts, offset_map):
    tiles = tile_values[0, 0]
    row_size = lax.axis_size("row")
    off_size = lax.axis_size("off")
    me = lax.axis_index("off").astype(jnp.int32)
    vectors, shard = start_block.shape
    slots, width, _ = tiles.shape
    blocks = shard // width
    total = shard * off_size * row_size
    count = len(pairs(vectors))
    parts = [vectors - vectors // 2, vectors // 2]
    row_bits, off_bits = bits_of("row")[::-1], bits_of("off")

    packed = call(
        functools.partial(pack_kernel, parts, blocks),
        tuple(jax.ShapeDtypeStruct((n * blocks, width), F32) for n in parts), (start_block,),
    )
    diagonal = diagonal.reshape(blocks, width)
    ids, offset, inner = call(
        functools.partial(prepare_kernel, parts, slots),
        (
            jax.ShapeDtypeStruct((8, width), jnp.int32),
            jax.ShapeDtypeStruct((1,), jnp.int32),
            jax.ShapeDtypeStruct((16 * count, width), F32),
        ),
        (me[None], tile_counts, offset_map, tile_rows[0], tile_cols[0], *packed, diagonal),
        [SMEM] * 3 + [VMEM] * (3 + len(parts)), out_specs=(VMEM, SMEM, VMEM),
    )
    offset = offset[0]
    steps = row_size // 2

    def routed(function, *operands):
        if steps <= 4:

            def branch(s):
                return functools.partial(function, lambda x, sign: shift(x, sign * s))

            return lax.switch(offset, [branch(s) for s in range(steps)], *operands)

        def move(x, sign):
            for b in range(steps.bit_length() - 1):
                x = jnp.where(offset >> b & 1 == 1, shift(x, sign << b), x)
            return x

        return function(move, *operands)

    group_ids = routed(lambda move, x: move(x, 1), ids)
    high, low = divide(tiles)

    def pick(k, hold):
        n = parts[k]
        pieces = gather_off({0: packed[k]}, off_bits, hold)
        picked = jax.ShapeDtypeStruct((n * slots, width), F32)
        return call(
            functools.partial(pick_kernel, n, slots, blocks), (picked, picked),
            (me[None], ids, group_ids, *pieces), [SMEM] * 3 + [VMEM] * off_size,
        )

    row0, col0 = pick(0, (group_ids, high, low))
    arrived0 = routed(lambda move, x: move(x, -1), col0)
    row1, col1 = pick(1, (arrived0,))

    def second(move, rows, arrived0, col1, high, low, ids):
        arrived = [arrived0, move(col1, -1)]
        mirrored, later = multiply(rows, high, low, ids, 1, parts, parts, False)
        returned = move(mirrored, 1)
        (direct,) = multiply(arrived, high, low, ids, 0, parts, [vectors], True)
        return direct, returned, later

    rows = [row0, row1]
    direct, returned, later = routed(second, rows, arrived0, col1, high, low, ids)
    sums = call(
        functools.partial(couple_kernel, parts, slots),
        jax.ShapeDtypeStruct((-(-2 * count // 8) * 8, width), F32), (*rows, direct, inner),
    )
    top = off_bits[0]
    partial_sums = sums
    sums = sum_step(sums, "off", top)
    direct_over = swap(after(direct, partial_sums), "off", top)
    returned_over = swap(after(returned, partial_sums), "off", top)

    def third(move, later, sums):
        returned = move(later, 1)
        for bit in row_bits[:-1]:
            sums = sum_step(sums, "row", bit)
        return returned, sums

    later, sums = routed(third, later, sums)
    later_over = swap(later, "off", top)
    sums = sum_step(sums, "row", row_bits[-1])
    direct = gather_off({0: direct, top: direct_over}, off_bits[1:])
    returned = gather_off({0: returned, top: returned_over}, off_bits[1:])
    later = gather_off({0: later, top: later_over}, off_bits[1:], (sums,))
    lists = []
    for a, b, c in zip(direct, returned, later):
        lists += [(a,), (b, c)]
    image = add_lists(me[None], lists[:off_size], slots, blocks)
    sums = after(sums, image)
    for bit in off_bits[1:]:
        sums = sum_step(sums, "off", bit)
    image = add_lists(me[None], lists[off_size:], slots, blocks, image)
    out = jax.ShapeDtypeStruct((vectors, shard), F32)
    return call(
        functools.partial(finish_kernel, parts, float(total)), (out, out),
        (sums, *packed, diagonal, image), limit=24,
        scratch=(
            pltpu.VMEM((8 * (vectors * vectors + count), width), F32),
            pltpu.VMEM((8 * blocks, width), F32),
            pltpu.VMEM((8 * blocks, width), F32),
        ),
    )


def solution(mesh):
    return jax.shard_map(
        body,
        mesh=mesh,
        in_specs=(
            P(None, ("row", "off")),
            P(("row", "off")),
            P("row", "off", None, None, None),
            P("row", "off", None),
            P("row", "off", None),
            P("row", "off"),
            P(),
        ),
        out_specs=(P(None, ("row", "off")), P(None, ("row", "off"))),
        check_vma=False,
    )
```

```python
import functools

import jax
import jax.numpy as jnp
from jax import lax
from jax.experimental import pallas as pl
from jax.experimental.pallas import tpu as pltpu
from jax.sharding import PartitionSpec as P

VMEM = pl.BlockSpec(memory_space=pltpu.VMEM)
SMEM = pl.BlockSpec(memory_space=pltpu.SMEM)
MIB = 1 << 20
BF16 = jnp.bfloat16
F32 = jnp.float32


def swap(x, axis, mask):
    n = lax.axis_size(axis)
    return lax.ppermute(x, axis, [(i, i ^ mask) for i in range(n)])


def shift(x, distance):
    n = lax.axis_size("row")
    return lax.ppermute(x, "row", [(i, (i + distance) % n) for i in range(n)])


def after(x, *others):
    return lax.optimization_barrier((x, *others))[0]


def bits_of(axis):
    return [1 << b for b in reversed(range(lax.axis_size(axis).bit_length() - 1))]


def gather_off(x, name, hold=()):
    pieces = {0: x}
    for level, bit in enumerate(bits_of("off")):
        for m in list(pieces):
            with jax.named_scope(f"{name}_{level}_{m}"):
                source = after(pieces[m], *hold) if m and hold else pieces[m]
                pieces[m | bit] = swap(source, "off", bit)
    return [pieces[m] for m in sorted(pieces)]


def sum_step(x, axis, bit, name):
    with jax.named_scope(name):
        return x + swap(x, axis, bit)


def pairs(vectors):
    return [(i, j) for i in range(vectors) for j in range(i + 1)]


def call(kernel, name, out_shape, operands, in_specs=None, limit=16, scratch=(), flops=0, **kw):
    many = isinstance(out_shape, tuple)
    moved = sum(x.size * x.dtype.itemsize for x in operands)
    return pl.pallas_call(
        kernel,
        out_shape=out_shape,
        in_specs=in_specs or [VMEM] * len(operands),
        out_specs=kw.pop("out_specs", (VMEM,) * len(out_shape) if many else VMEM),
        scratch_shapes=list(scratch),
        compiler_params=pltpu.CompilerParams(vmem_limit_bytes=limit * MIB),
        cost_estimate=pl.CostEstimate(flops=flops, bytes_accessed=moved, transcendentals=0),
        name=name,
        **kw,
    )(*operands)


def pack_kernel(vectors, blocks, x_ref, o_ref):
    width = o_ref.shape[-1]

    @pl.loop(0, blocks, unroll=8)
    def _(b):
        o_ref[pl.ds(b * vectors, vectors), :] = x_ref[:, pl.ds(pl.multiple_of(b * width, width), width)]


def inner_kernel(vectors, x_ref, d_ref, o_ref):
    blocks, width = d_ref.shape
    both = pairs(vectors)
    zero = jnp.zeros((8, width), F32)

    def step(c, sums):
        at = pl.multiple_of(c * 8, 8)
        d = d_ref[pl.ds(at, 8), :]
        x = [x_ref[pl.ds(at * vectors + v, 8, stride=vectors), :] for v in range(vectors)]
        y = [a * d for a in x]
        first = [s + x[i] * x[j] for s, (i, j) in zip(sums, both)]
        second = [s + x[i] * y[j] for s, (i, j) in zip(sums[len(both) :], both)]
        return tuple(first + second)

    sums = lax.fori_loop(0, blocks // 8, step, (zero,) * (2 * len(both)))
    for k, s in enumerate(sums):
        o_ref[pl.ds(8 * k, 8), :] = s


def divide_kernel(t_ref, hi_ref, lo_ref):
    t = t_ref[...]
    hi = t.astype(BF16)
    hi_ref[...] = hi
    lo_ref[...] = (t - hi.astype(F32)).astype(BF16)


def divide(tiles):
    slots, width, _ = tiles.shape
    step = max(s for s in (1, 2, 4, 8) if slots % s == 0)
    spec = pl.BlockSpec((step, width, width), lambda i: (i, 0, 0))
    shape = jax.ShapeDtypeStruct(tiles.shape, BF16)
    return call(
        divide_kernel, "divide", (shape, shape), (tiles,), [spec], 8,
        flops=tiles.size * 4, grid=(slots // step,), out_specs=(spec, spec),
    )


def pick_kernel(vectors, slots, where_ref, at_ref, *refs):
    pieces, outs = refs[:-2], refs[-2:]
    for which, out in enumerate(outs):

        @pl.loop(0, slots, unroll=4)
        def _(t):
            m = where_ref[which, t]
            at = at_ref[which, t]
            value = jnp.zeros((vectors, out.shape[-1]), F32)
            for k, piece in enumerate(pieces):
                value = jnp.where(m == k, piece[pl.ds(at, vectors), :], value)
            out[pl.ds(t * vectors, vectors), :] = value


def multiply_kernel(vectors, step, transposed, x_ref, hi_ref, lo_ref, o_ref):
    base = pl.program_id(0) * step
    width = x_ref.shape[-1]
    dims = (((1,), (1 if transposed else 0,)), ((), ()))

    def left(t):
        x = x_ref[pl.ds(t * vectors, vectors), :]
        x = jnp.concatenate([x, jnp.zeros((8 - vectors, width), F32)], axis=0)
        hi = x.astype(BF16).astype(F32)
        lo = x - hi
        top = jnp.concatenate([hi, hi], axis=1)
        low = jnp.concatenate([lo, jnp.zeros_like(lo)], axis=1)
        return [top, low]

    @pl.loop(0, step // 2, unroll=2)
    def _(p):
        i = 2 * p
        x = jnp.concatenate(left(base + i) + left(base + i + 1), axis=0).astype(BF16)
        along, across = (1, 0) if transposed else (0, 1)
        t = [jnp.concatenate([hi_ref[i + k], lo_ref[i + k]], axis=along) for k in (0, 1)]
        y = lax.dot_general(x, jnp.concatenate(t, axis=across), dims, preferred_element_type=F32)
        o_ref[pl.ds((base + i) * vectors, vectors), :] = (y[0:8, :width] + y[8:16, :width])[:vectors]
        o_ref[pl.ds((base + i + 1) * vectors, vectors), :] = (y[16:24, width:] + y[24:32, width:])[:vectors]


def multiply(x, high, low, ids, vectors, transposed, coupled=None):
    slots, width, _ = high.shape
    step = max(s for s in (2, 4, 8, 16, 20) if slots % s == 0)
    rows = vectors * slots
    spec = pl.BlockSpec((step, width, width), lambda i: (i, 0, 0))
    count = len(pairs(vectors))

    def kernel(x_ref, hi_ref, lo_ref, ids_ref, *refs):
        o_ref = refs[2] if coupled else refs[0]
        multiply_kernel(vectors, step, transposed, x_ref, hi_ref, lo_ref, o_ref)
        o_ref[pl.ds(rows, 8), :] = ids_ref[...]
        if coupled:

            @pl.when(pl.program_id(0) == pl.num_programs(0) - 1)
            def _():
                couple(vectors, slots, refs[0], o_ref, refs[1], refs[3])
                refs[4][...] = refs[3][...]

    out = jax.ShapeDtypeStruct((rows + 8, width), F32)
    if coupled:
        sums = jax.ShapeDtypeStruct((-(-2 * count // 8) * 8, width), F32)
        out = (out, sums, sums)
    operands = (x, high, low, ids) + (coupled or ())
    return call(
        kernel, "multiply", out, operands, [VMEM, spec, spec] + [VMEM] * (len(operands) - 3), 12,
        flops=slots * 2 * 32 * 256 * 128, grid=(slots // step,),
    )


def couple(vectors, slots, x_ref, y_ref, p_ref, o_ref):
    both = pairs(vectors)
    n = len(both)

    def step(c, sums):
        at = pl.multiple_of(8 * c * vectors, 8)
        x = [x_ref[pl.ds(at + v, 8, stride=vectors), :] for v in range(vectors)]
        y = [y_ref[pl.ds(at + v, 8, stride=vectors), :] for v in range(vectors)]
        return tuple(s + (x[i] * y[j] + x[j] * y[i]) for s, (i, j) in zip(sums, both))

    sums = tuple(p_ref[pl.ds(8 * (n + k), 8), :] for k in range(n))
    sums = lax.fori_loop(0, slots // 8, step, sums)
    sums = [p_ref[pl.ds(8 * k, 8), :] for k in range(n)] + list(sums)
    for k, s in enumerate(sums):
        o_ref[k : k + 1, :] = jnp.sum(s, axis=0, keepdims=True)
    if o_ref.shape[0] > 2 * n:
        o_ref[2 * n :, :] = jnp.zeros((o_ref.shape[0] - 2 * n, o_ref.shape[1]), F32)
    total = jnp.sum(o_ref[...], axis=1, keepdims=True)
    o_ref[...] = jnp.broadcast_to(total, o_ref.shape)


def add_kernel(vectors, slots, blocks, started, me_ref, *refs):
    o_ref, lists = refs[-1], refs[:-1]
    if started:
        before, lists = lists[0], lists[1:]
    width = o_ref.shape[-1]
    row = lax.broadcasted_iota(jnp.int32, (blocks, width), 0) + me_ref[0] * blocks
    row = row.astype(F32)
    pad = jnp.zeros((width - slots, vectors * width), F32)
    sums = None
    for k in range(0, len(lists), 2):
        hots, blocks_of = [], []
        for ref in lists[k : k + 2]:
            ids = ref[vectors * slots : vectors * slots + 1, :]
            hots.append(jnp.where(ids == row, 1.0, 0.0).astype(BF16))
            y = [ref[pl.ds(v, slots, stride=vectors), :] for v in range(vectors)]
            blocks_of += [jnp.concatenate(y, axis=1), pad]
        hot = jnp.concatenate(hots, axis=1)
        y = jnp.concatenate(blocks_of, axis=0)
        hi = y.astype(BF16)
        lo = (y - hi.astype(F32)).astype(BF16)
        part = jnp.dot(hot, hi, preferred_element_type=F32) + jnp.dot(hot, lo, preferred_element_type=F32)
        sums = part if sums is None else sums + part
    for v in range(vectors):
        s = sums[:, v * width : (v + 1) * width]
        if started:
            s = s + before[pl.ds(v * blocks, blocks), :]
        o_ref[pl.ds(v * blocks, blocks), :] = s


def add_lists(me, lists, vectors, slots, blocks, before=None):
    width = lists[0].shape[-1]
    operands = (me,) + (() if before is None else (before,)) + tuple(lists)
    return call(
        functools.partial(add_kernel, vectors, slots, blocks, before is not None),
        "add_lists", jax.ShapeDtypeStruct((vectors * blocks, width), F32), operands,
        [SMEM] + [VMEM] * (len(operands) - 1), 16, flops=len(lists) * 2 * 256 * 256 * 768,
    )


def algebra(vectors, total, sums_ref):
    both = pairs(vectors)
    n = len(both)
    g, q = {}, {}
    for k, (i, j) in enumerate(both):
        g[i, j] = sums_ref[k : k + 1, :] * (1.0 / total)
        q[i, j] = q[j, i] = sums_ref[n + k : n + k + 1, :] * (1.0 / total)
    low, inv = {}, {}
    rev = []
    for j in range(vectors):
        s = g[j, j]
        for k in range(j):
            s = s - low[j, k] * low[j, k]
        rev.append(1.0 / jnp.sqrt(s))
        for i in range(j + 1, vectors):
            s = g[i, j]
            for k in range(j):
                s = s - low[i, k] * low[j, k]
            low[i, j] = s * rev[j]
    for j in range(vectors):
        inv[j, j] = rev[j]
        for i in range(j + 1, vectors):
            s = low[i, j] * inv[j, j]
            for k in range(j + 1, i):
                s = s + low[i, k] * inv[k, j]
            inv[i, j] = -s * rev[i]
    half, onto, proj = {}, {}, {}
    for i in range(vectors):
        for j in range(vectors):
            half[i, j] = sum(inv[i, k] * q[k, j] for k in range(i + 1))
    for i in range(vectors):
        for j in range(vectors):
            proj[i, j] = sum(half[i, k] * inv[j, k] for k in range(j + 1))
    for i in range(vectors):
        for j in range(vectors):
            onto[i, j] = sum(proj[i, k] * inv[k, j] for k in range(j, vectors))
    return inv, onto


def finish_kernel(vectors, total, sums_ref, x_ref, d_ref, m_ref, final_ref, residual_ref, coef, res, fin):
    blocks, width = d_ref.shape
    inv, onto = algebra(vectors, total, sums_ref)
    places = {}
    for name, table in (("i", inv), ("o", onto)):
        for key in sorted(table):
            k = len(places)
            places[name, key] = k
            coef[pl.ds(8 * k, 8), :] = jnp.broadcast_to(table[key], (8, width))

    @pl.loop(0, blocks // 8, unroll=2)
    def _(c):
        at = pl.multiple_of(c * 8, 8)
        d = d_ref[pl.ds(at, 8), :]
        rd = 1.0 / d
        x = [x_ref[pl.ds(at * vectors + v, 8, stride=vectors), :] for v in range(vectors)]
        m = [m_ref[pl.ds(v * blocks + at, 8), :] + x[v] * d for v in range(vectors)]

        def value(name, i, j):
            return coef[pl.ds(8 * places[name, (i, j)], 8), :]

        for i in range(vectors):
            basis = r = None
            for j in range(i + 1):
                f = value("i", i, j)
                basis = f * x[j] if basis is None else basis + f * x[j]
                r = f * m[j] if r is None else r + f * m[j]
            for j in range(vectors):
                r = r - value("o", i, j) * x[j]
            res[pl.ds(8 * at + i, 8, stride=8), :] = r
            fin[pl.ds(8 * at + i, 8, stride=8), :] = basis - r * rd

    @pl.loop(0, blocks, unroll=8)
    def _(b):
        at = pl.multiple_of(b * width, width)
        residual_ref[:, pl.ds(at, width)] = res[pl.ds(pl.multiple_of(8 * b, 8), vectors), :]
        final_ref[:, pl.ds(at, width)] = fin[pl.ds(pl.multiple_of(8 * b, 8), vectors), :]


def body(start_block, diagonal, tile_values, tile_rows, tile_cols, tile_counts, offset_map):
    tiles = tile_values[0, 0]
    live_count = tile_counts[0, 0]
    row_size = lax.axis_size("row")
    off_size = lax.axis_size("off")
    me = lax.axis_index("off").astype(jnp.int32)
    offset = offset_map[me]
    vectors, shard = start_block.shape
    slots, width, _ = tiles.shape
    blocks = shard // width
    total = shard * off_size * row_size
    distances = range(row_size // 2)
    count = len(pairs(vectors))

    packed = call(
        functools.partial(pack_kernel, vectors, blocks), "pack",
        jax.ShapeDtypeStruct((vectors * blocks, width), F32), (start_block,),
    )
    live = jnp.arange(slots, dtype=jnp.int32) < live_count
    row_ids = jnp.where(live, tile_rows[0, 0], -1)
    col_ids = jnp.where(live, tile_cols[0, 0], -1)

    def padded(ids):
        return jnp.pad(ids.astype(F32)[None, :], ((0, 7), (0, width - slots)), constant_values=-1)

    row_line, col_line = padded(row_ids), padded(col_ids)
    group_line = lax.switch(
        offset,
        [functools.partial(lambda s, c: shift(c, s) if s else c, s) for s in distances],
        col_line,
    )
    both = jnp.stack([row_ids, group_line[0, :slots].astype(jnp.int32)])
    where = jnp.where(both < 0, -1, (both // blocks) ^ me)
    at = jnp.where(both < 0, 0, both % blocks) * vectors

    diagonal = diagonal.reshape(blocks, width)
    inner = call(
        functools.partial(inner_kernel, vectors), "inner",
        jax.ShapeDtypeStruct((16 * count, width), F32), (packed, diagonal),
    )
    high, low = divide(tiles)
    pieces = gather_off(packed, "pieces", (where, at, inner, high, low))
    picked = jax.ShapeDtypeStruct((vectors * slots, width), F32)
    picked_row, picked_col = call(
        functools.partial(pick_kernel, vectors, slots), "pick", (picked, picked),
        (where, at, *pieces), [SMEM, SMEM] + [VMEM] * off_size,
    )

    row_bits, off_bits = bits_of("row")[::-1], bits_of("off")[::-1]

    def middle(s, picked_row, picked_col, high, low, row_line, col_line, inner):
        with jax.named_scope("columns"):
            arrived = shift(picked_col, -s) if s else picked_col
        mirrored = multiply(picked_row, high, low, col_line, vectors, False)
        with jax.named_scope("products"):
            mirrored = after(mirrored, arrived)
            returned = shift(mirrored, s) if s else mirrored
        direct, sums, again = multiply(arrived, high, low, row_line, vectors, True, (picked_row, inner))
        with jax.named_scope("first"):
            sums = again + swap(sums, "row", row_bits[0])
        sums = sum_step(sums, "row", row_bits[1], "second")
        return direct, returned, sums

    direct, returned, sums = lax.switch(
        offset,
        [functools.partial(middle, s) for s in distances],
        picked_row, picked_col, high, low, row_line, col_line, inner,
    )
    stages = [sums]
    order = [("row", b) for b in row_bits[2:]] + [("off", b) for b in off_bits]
    for k, (axis, bit) in enumerate(order[:-1]):
        stages.append(sum_step(stages[-1], axis, bit, f"sum_{k}"))
    lists = []
    for a, b in zip(
        gather_off(direct, "direct", (stages[-2],)), gather_off(returned, "returned", (stages[-1],))
    ):
        lists += [a, b]
    half = off_size
    image = add_lists(me[None], lists[:half], vectors, slots, blocks)
    sums = sum_step(after(stages[-1], image), *order[-1], "sum_end")
    image = add_lists(me[None], lists[half:], vectors, slots, blocks, image)
    out = jax.ShapeDtypeStruct((vectors, shard), F32)
    return call(
        functools.partial(finish_kernel, vectors, float(total)), "finish", (out, out),
        (sums, packed, diagonal, image), limit=24,
        scratch=(
            pltpu.VMEM((8 * (vectors * vectors + count), width), F32),
            pltpu.VMEM((8 * blocks, width), F32),
            pltpu.VMEM((8 * blocks, width), F32),
        ),
    )


def solution(mesh):
    return jax.shard_map(
        body,
        mesh=mesh,
        in_specs=(
            P(None, ("row", "off")),
            P(("row", "off")),
            P("row", "off", None, None, None),
            P("row", "off", None),
            P("row", "off", None),
            P("row", "off"),
            P(),
        ),
        out_specs=(P(None, ("row", "off")), P(None, ("row", "off"))),
        check_vma=False,
    )
```

```python
import functools

import jax
import jax.numpy as jnp
from jax import lax
from jax.experimental import pallas as pl
from jax.experimental.pallas import tpu as pltpu
from jax.sharding import PartitionSpec as P


VMEM = pl.BlockSpec(memory_space=pltpu.VMEM)
SMEM = pl.BlockSpec(memory_space=pltpu.SMEM)
MIB = 1 << 20
BF16 = jnp.bfloat16
F32 = jnp.float32


def swap(x, axis, mask):
    n = lax.axis_size(axis)
    return lax.ppermute(x, axis, [(i, i ^ mask) for i in range(n)])


def shift(x, distance):
    n = lax.axis_size("row")
    return lax.ppermute(x, "row", [(i, (i + distance) % n) for i in range(n)])


def after(x, *others):
    return lax.optimization_barrier((x, *others))[0]


def bits_of(axis):
    return [1 << b for b in reversed(range(lax.axis_size(axis).bit_length() - 1))]


def gather_off(x, hold=()):
    pieces = {0: x}
    for bit in bits_of("off"):
        for m in list(pieces):
            source = after(pieces[m], *hold) if m and hold else pieces[m]
            pieces[m | bit] = swap(source, "off", bit)
    return [pieces[m] for m in sorted(pieces)]


def sum_step(x, axis, bit):
    return x + swap(x, axis, bit)


def pairs(vectors):
    return [(i, j) for i in range(vectors) for j in range(i + 1)]


def call(kernel, out_shape, operands, in_specs=None, limit=16, scratch=(), flops=0, **kw):
    many = isinstance(out_shape, tuple)
    moved = sum(x.size * x.dtype.itemsize for x in operands)
    return pl.pallas_call(
        kernel,
        out_shape=out_shape,
        in_specs=in_specs or [VMEM] * len(operands),
        out_specs=kw.pop("out_specs", (VMEM,) * len(out_shape) if many else VMEM),
        scratch_shapes=list(scratch),
        compiler_params=pltpu.CompilerParams(vmem_limit_bytes=limit * MIB),
        cost_estimate=pl.CostEstimate(flops=flops, bytes_accessed=moved, transcendentals=0),
        **kw,
    )(*operands)


def pack_kernel(vectors, blocks, x_ref, o_ref):
    width = o_ref.shape[-1]

    @pl.loop(0, blocks, unroll=8)
    def _(b):
        o_ref[pl.ds(b * vectors, vectors), :] = x_ref[:, pl.ds(pl.multiple_of(b * width, width), width)]


def inner_kernel(vectors, x_ref, d_ref, o_ref):
    blocks, width = d_ref.shape
    both = pairs(vectors)
    zero = jnp.zeros((8, width), F32)

    def step(c, sums):
        at = pl.multiple_of(c * 8, 8)
        d = d_ref[pl.ds(at, 8), :]
        x = [x_ref[pl.ds(at * vectors + v, 8, stride=vectors), :] for v in range(vectors)]
        y = [a * d for a in x]
        first = [s + x[i] * x[j] for s, (i, j) in zip(sums, both)]
        second = [s + x[i] * y[j] for s, (i, j) in zip(sums[len(both) :], both)]
        return tuple(first + second)

    sums = lax.fori_loop(0, blocks // 8, step, (zero,) * (2 * len(both)))
    for k, s in enumerate(sums):
        o_ref[pl.ds(8 * k, 8), :] = s


def divide_kernel(t_ref, hi_ref, lo_ref):
    t = t_ref[...]
    hi = t.astype(BF16)
    hi_ref[...] = hi
    lo_ref[...] = (t - hi.astype(F32)).astype(BF16)


def divide(tiles):
    slots, width, _ = tiles.shape
    step = max(s for s in (1, 2, 4, 8) if slots % s == 0)
    spec = pl.BlockSpec((step, width, width), lambda i: (i, 0, 0))
    shape = jax.ShapeDtypeStruct(tiles.shape, BF16)
    return call(
        divide_kernel, (shape, shape), (tiles,), [spec], 8,
        flops=tiles.size * 4, grid=(slots // step,), out_specs=(spec, spec),
    )


def pick_kernel(vectors, slots, where_ref, at_ref, *refs):
    pieces, outs = refs[:-2], refs[-2:]
    for which, out in enumerate(outs):

        @pl.loop(0, slots, unroll=4)
        def _(t):
            m = where_ref[which, t]
            at = at_ref[which, t]
            value = jnp.zeros((vectors, out.shape[-1]), F32)
            for k, piece in enumerate(pieces):
                value = jnp.where(m == k, piece[pl.ds(at, vectors), :], value)
            out[pl.ds(t * vectors, vectors), :] = value


def multiply_kernel(vectors, step, transposed, x_ref, hi_ref, lo_ref, o_ref):
    base = pl.program_id(0) * step
    width = x_ref.shape[-1]
    dims = (((1,), (1 if transposed else 0,)), ((), ()))

    def left(t):
        x = x_ref[pl.ds(t * vectors, vectors), :]
        x = jnp.concatenate([x, jnp.zeros((8 - vectors, width), F32)], axis=0)
        hi = x.astype(BF16).astype(F32)
        lo = x - hi
        top = jnp.concatenate([hi, hi], axis=1)
        low = jnp.concatenate([lo, jnp.zeros_like(lo)], axis=1)
        return [top, low]

    @pl.loop(0, step // 2, unroll=2)
    def _(p):
        i = 2 * p
        x = jnp.concatenate(left(base + i) + left(base + i + 1), axis=0).astype(BF16)
        along, across = (1, 0) if transposed else (0, 1)
        t = [jnp.concatenate([hi_ref[i + k], lo_ref[i + k]], axis=along) for k in (0, 1)]
        y = lax.dot_general(x, jnp.concatenate(t, axis=across), dims, preferred_element_type=F32)
        o_ref[pl.ds((base + i) * vectors, vectors), :] = (y[0:8, :width] + y[8:16, :width])[:vectors]
        o_ref[pl.ds((base + i + 1) * vectors, vectors), :] = (y[16:24, width:] + y[24:32, width:])[:vectors]


def multiply(x, high, low, ids, vectors, transposed, coupled=None):
    slots, width, _ = high.shape
    step = max(s for s in (2, 4, 8, 16, 20) if slots % s == 0)
    rows = vectors * slots
    spec = pl.BlockSpec((step, width, width), lambda i: (i, 0, 0))
    count = len(pairs(vectors))

    def kernel(x_ref, hi_ref, lo_ref, ids_ref, *refs):
        o_ref = refs[2] if coupled else refs[0]
        multiply_kernel(vectors, step, transposed, x_ref, hi_ref, lo_ref, o_ref)
        o_ref[pl.ds(rows, 8), :] = ids_ref[...]
        if coupled:

            @pl.when(pl.program_id(0) == pl.num_programs(0) - 1)
            def _():
                couple(vectors, slots, refs[0], o_ref, refs[1], refs[3])
                refs[4][...] = refs[3][...]

    out = jax.ShapeDtypeStruct((rows + 8, width), F32)
    if coupled:
        sums = jax.ShapeDtypeStruct((-(-2 * count // 8) * 8, width), F32)
        out = (out, sums, sums)
    operands = (x, high, low, ids) + (coupled or ())
    return call(
        kernel, out, operands, [VMEM, spec, spec] + [VMEM] * (len(operands) - 3), 12,
        flops=slots * 2 * 32 * 256 * 128, grid=(slots // step,),
    )


def couple(vectors, slots, x_ref, y_ref, p_ref, o_ref):
    both = pairs(vectors)
    n = len(both)

    def step(c, sums):
        at = pl.multiple_of(8 * c * vectors, 8)
        x = [x_ref[pl.ds(at + v, 8, stride=vectors), :] for v in range(vectors)]
        y = [y_ref[pl.ds(at + v, 8, stride=vectors), :] for v in range(vectors)]
        return tuple(s + (x[i] * y[j] + x[j] * y[i]) for s, (i, j) in zip(sums, both))

    sums = tuple(p_ref[pl.ds(8 * (n + k), 8), :] for k in range(n))
    sums = lax.fori_loop(0, slots // 8, step, sums)
    sums = [p_ref[pl.ds(8 * k, 8), :] for k in range(n)] + list(sums)
    for k, s in enumerate(sums):
        o_ref[k : k + 1, :] = jnp.sum(s, axis=0, keepdims=True)
    if o_ref.shape[0] > 2 * n:
        o_ref[2 * n :, :] = jnp.zeros((o_ref.shape[0] - 2 * n, o_ref.shape[1]), F32)
    total = jnp.sum(o_ref[...], axis=1, keepdims=True)
    o_ref[...] = jnp.broadcast_to(total, o_ref.shape)


def add_kernel(vectors, slots, blocks, started, me_ref, *refs):
    o_ref, lists = refs[-1], refs[:-1]
    if started:
        before, lists = lists[0], lists[1:]
    width = o_ref.shape[-1]
    row = lax.broadcasted_iota(jnp.int32, (blocks, width), 0) + me_ref[0] * blocks
    row = row.astype(F32)
    pad = jnp.zeros((width - slots, vectors * width), F32)
    sums = None
    for k in range(0, len(lists), 2):
        hots, blocks_of = [], []
        for ref in lists[k : k + 2]:
            ids = ref[vectors * slots : vectors * slots + 1, :]
            hots.append(jnp.where(ids == row, 1.0, 0.0).astype(BF16))
            y = [ref[pl.ds(v, slots, stride=vectors), :] for v in range(vectors)]
            blocks_of += [jnp.concatenate(y, axis=1), pad]
        hot = jnp.concatenate(hots, axis=1)
        y = jnp.concatenate(blocks_of, axis=0)
        hi = y.astype(BF16)
        lo = (y - hi.astype(F32)).astype(BF16)
        part = jnp.dot(hot, hi, preferred_element_type=F32) + jnp.dot(hot, lo, preferred_element_type=F32)
        sums = part if sums is None else sums + part
    for v in range(vectors):
        s = sums[:, v * width : (v + 1) * width]
        if started:
            s = s + before[pl.ds(v * blocks, blocks), :]
        o_ref[pl.ds(v * blocks, blocks), :] = s


def add_lists(me, lists, vectors, slots, blocks, before=None):
    width = lists[0].shape[-1]
    operands = (me,) + (() if before is None else (before,)) + tuple(lists)
    return call(
        functools.partial(add_kernel, vectors, slots, blocks, before is not None),
        jax.ShapeDtypeStruct((vectors * blocks, width), F32), operands,
        [SMEM] + [VMEM] * (len(operands) - 1), 16, flops=len(lists) * 2 * 256 * 256 * 768,
    )


def algebra(vectors, total, sums_ref):
    both = pairs(vectors)
    n = len(both)
    g, q = {}, {}
    for k, (i, j) in enumerate(both):
        g[i, j] = sums_ref[k : k + 1, :] * (1.0 / total)
        q[i, j] = q[j, i] = sums_ref[n + k : n + k + 1, :] * (1.0 / total)
    low, inv = {}, {}
    rev = []
    for j in range(vectors):
        s = g[j, j]
        for k in range(j):
            s = s - low[j, k] * low[j, k]
        rev.append(1.0 / jnp.sqrt(s))
        for i in range(j + 1, vectors):
            s = g[i, j]
            for k in range(j):
                s = s - low[i, k] * low[j, k]
            low[i, j] = s * rev[j]
    for j in range(vectors):
        inv[j, j] = rev[j]
        for i in range(j + 1, vectors):
            s = low[i, j] * inv[j, j]
            for k in range(j + 1, i):
                s = s + low[i, k] * inv[k, j]
            inv[i, j] = -s * rev[i]
    half, onto, proj = {}, {}, {}
    for i in range(vectors):
        for j in range(vectors):
            half[i, j] = sum(inv[i, k] * q[k, j] for k in range(i + 1))
    for i in range(vectors):
        for j in range(vectors):
            proj[i, j] = sum(half[i, k] * inv[j, k] for k in range(j + 1))
    for i in range(vectors):
        for j in range(vectors):
            onto[i, j] = sum(proj[i, k] * inv[k, j] for k in range(j, vectors))
    return inv, onto


def finish_kernel(vectors, total, steps, sums_ref, x_ref, d_ref, m_ref, final_ref, residual_ref, coef, res, fin):
    blocks, width = d_ref.shape
    chunk = blocks // steps
    start = pl.program_id(0) * chunk
    both = pairs(vectors)
    places = {("i", key): k for k, key in enumerate(both)}
    for i in range(vectors):
        for j in range(vectors):
            places["o", (i, j)] = len(places)

    @pl.when(pl.program_id(0) == 0)
    def _():
        inv, onto = algebra(vectors, total, sums_ref)
        for name, table in (("i", inv), ("o", onto)):
            for key in table:
                coef[pl.ds(8 * places[name, key], 8), :] = jnp.broadcast_to(table[key], (8, width))

    @pl.loop(0, chunk // 8, unroll=2)
    def _(c):
        local = pl.multiple_of(c * 8, 8)
        at = pl.multiple_of(start + local, 8)
        d = d_ref[pl.ds(at, 8), :]
        rd = 1.0 / d
        x = [x_ref[pl.ds(at * vectors + v, 8, stride=vectors), :] for v in range(vectors)]
        m = [m_ref[pl.ds(v * blocks + at, 8), :] + x[v] * d for v in range(vectors)]

        def value(name, i, j):
            return coef[pl.ds(8 * places[name, (i, j)], 8), :]

        for i in range(vectors):
            basis = r = None
            for j in range(i + 1):
                f = value("i", i, j)
                basis = f * x[j] if basis is None else basis + f * x[j]
                r = f * m[j] if r is None else r + f * m[j]
            for j in range(vectors):
                r = r - value("o", i, j) * x[j]
            res[pl.ds(8 * local + i, 8, stride=8), :] = r
            fin[pl.ds(8 * local + i, 8, stride=8), :] = basis - r * rd

    @pl.loop(0, chunk, unroll=8)
    def _(b):
        at = pl.multiple_of(b * width, width)
        residual_ref[:, pl.ds(at, width)] = res[pl.ds(pl.multiple_of(8 * b, 8), vectors), :]
        final_ref[:, pl.ds(at, width)] = fin[pl.ds(pl.multiple_of(8 * b, 8), vectors), :]


def body(start_block, diagonal, tile_values, tile_rows, tile_cols, tile_counts, offset_map):
    tiles = tile_values[0, 0]
    live_count = tile_counts[0, 0]
    row_size = lax.axis_size("row")
    off_size = lax.axis_size("off")
    me = lax.axis_index("off").astype(jnp.int32)
    offset = offset_map[me]
    vectors, shard = start_block.shape
    slots, width, _ = tiles.shape
    blocks = shard // width
    total = shard * off_size * row_size
    distances = range(row_size // 2)
    count = len(pairs(vectors))

    packed = call(
        functools.partial(pack_kernel, vectors, blocks),
        jax.ShapeDtypeStruct((vectors * blocks, width), F32), (start_block,),
    )
    live = jnp.arange(slots, dtype=jnp.int32) < live_count
    row_ids = jnp.where(live, tile_rows[0, 0], -1)
    col_ids = jnp.where(live, tile_cols[0, 0], -1)

    def padded(ids):
        return jnp.pad(ids.astype(F32)[None, :], ((0, 7), (0, width - slots)), constant_values=-1)

    row_line, col_line = padded(row_ids), padded(col_ids)
    group_line = lax.switch(
        offset,
        [functools.partial(lambda s, c: shift(c, s) if s else c, s) for s in distances],
        col_line,
    )
    both = jnp.stack([row_ids, group_line[0, :slots].astype(jnp.int32)])
    where = jnp.where(both < 0, -1, (both // blocks) ^ me)
    at = jnp.where(both < 0, 0, both % blocks) * vectors

    diagonal = diagonal.reshape(blocks, width)
    inner = call(
        functools.partial(inner_kernel, vectors),
        jax.ShapeDtypeStruct((16 * count, width), F32), (packed, diagonal),
    )
    high, low = divide(tiles)
    pieces = gather_off(packed, (where, at, inner, high, low))
    picked = jax.ShapeDtypeStruct((vectors * slots, width), F32)
    picked_row, picked_col = call(
        functools.partial(pick_kernel, vectors, slots), (picked, picked),
        (where, at, *pieces), [SMEM, SMEM] + [VMEM] * off_size,
    )

    row_bits, off_bits = bits_of("row")[::-1], bits_of("off")[::-1]

    def middle(s, picked_row, picked_col, high, low, row_line, col_line, inner):
        arrived = shift(picked_col, -s) if s else picked_col
        mirrored = multiply(picked_row, high, low, col_line, vectors, False)
        returned = shift(mirrored, s) if s else mirrored
        direct, sums, _ = multiply(arrived, high, low, row_line, vectors, True, (picked_row, inner))
        return direct, returned, sums

    direct, returned, sums = lax.switch(
        offset,
        [functools.partial(middle, s) for s in distances],
        picked_row, picked_col, high, low, row_line, col_line, inner,
    )
    stages = [sums]
    order = [("off", off_bits[-1])] + [("row", b) for b in row_bits] + [("off", b) for b in off_bits[:-1]]
    for axis, bit in order[:-1]:
        stages.append(sum_step(stages[-1], axis, bit))
    lists = []
    for a, b in zip(gather_off(direct, (stages[-2],)), gather_off(returned, (stages[-1],))):
        lists += [a, b]
    half = off_size
    image = add_lists(me[None], lists[:half], vectors, slots, blocks)
    sums = sum_step(stages[-1], *order[-1])
    image = add_lists(me[None], lists[half:], vectors, slots, blocks, image)
    out = jax.ShapeDtypeStruct((vectors, shard), F32)
    steps = 4 if blocks % 64 == 0 else 1
    spec = pl.BlockSpec((vectors, shard // steps), lambda i: (0, i))
    return call(
        functools.partial(finish_kernel, vectors, float(total), steps), (out, out),
        (sums, packed, diagonal, image), limit=24,
        scratch=(
            pltpu.VMEM((8 * (vectors * vectors + count), width), F32),
            pltpu.VMEM((8 * blocks // steps, width), F32),
            pltpu.VMEM((8 * blocks // steps, width), F32),
        ),
        grid=(steps,), out_specs=(spec, spec),
    )


def solution(mesh):
    return jax.shard_map(
        body,
        mesh=mesh,
        in_specs=(
            P(None, ("row", "off")),
            P(("row", "off")),
            P("row", "off", None, None, None),
            P("row", "off", None),
            P("row", "off", None),
            P("row", "off"),
            P(),
        ),
        out_specs=(P(None, ("row", "off")), P(None, ("row", "off"))),
        check_vma=False,
    )
```

```python
import functools

import jax
import jax.numpy as jnp
from jax import lax
from jax.experimental import pallas as pl
from jax.experimental.pallas import tpu as pltpu
from jax.sharding import PartitionSpec as P


VMEM = pl.BlockSpec(memory_space=pltpu.VMEM)
SMEM = pl.BlockSpec(memory_space=pltpu.SMEM)
MIB = 1 << 20
BF16 = jnp.bfloat16
F32 = jnp.float32


def swap(x, axis, mask):
    n = lax.axis_size(axis)
    return lax.ppermute(x, axis, [(i, i ^ mask) for i in range(n)])


def shift(x, distance):
    n = lax.axis_size("row")
    return lax.ppermute(x, "row", [(i, (i + distance) % n) for i in range(n)])


def after(x, *others):
    return lax.optimization_barrier((x, *others))[0]


def bits_of(axis):
    return [1 << b for b in reversed(range(lax.axis_size(axis).bit_length() - 1))]


def gather_off(x, hold=()):
    pieces = {0: x}
    for bit in bits_of("off"):
        for m in list(pieces):
            source = after(pieces[m], *hold) if m and hold else pieces[m]
            pieces[m | bit] = swap(source, "off", bit)
    return [pieces[m] for m in sorted(pieces)]


def sum_step(x, axis, bit):
    return x + swap(x, axis, bit)


def pairs(vectors):
    return [(i, j) for i in range(vectors) for j in range(i + 1)]


def call(kernel, out_shape, operands, in_specs=None, limit=16, scratch=(), flops=0, **kw):
    many = isinstance(out_shape, tuple)
    moved = sum(x.size * x.dtype.itemsize for x in operands)
    return pl.pallas_call(
        kernel,
        out_shape=out_shape,
        in_specs=in_specs or [VMEM] * len(operands),
        out_specs=kw.pop("out_specs", (VMEM,) * len(out_shape) if many else VMEM),
        scratch_shapes=list(scratch),
        compiler_params=pltpu.CompilerParams(vmem_limit_bytes=limit * MIB),
        cost_estimate=pl.CostEstimate(flops=flops, bytes_accessed=moved, transcendentals=0),
        **kw,
    )(*operands)


def pack_kernel(vectors, blocks, x_ref, o_ref):
    width = o_ref.shape[-1]

    @pl.loop(0, blocks, unroll=8)
    def _(b):
        o_ref[pl.ds(b * vectors, vectors), :] = x_ref[:, pl.ds(pl.multiple_of(b * width, width), width)]


def inner_kernel(vectors, x_ref, d_ref, o_ref):
    blocks, width = d_ref.shape
    both = pairs(vectors)
    zero = jnp.zeros((8, width), F32)

    def step(c, sums):
        at = pl.multiple_of(c * 8, 8)
        d = d_ref[pl.ds(at, 8), :]
        x = [x_ref[pl.ds(at * vectors + v, 8, stride=vectors), :] for v in range(vectors)]
        y = [a * d for a in x]
        first = [s + x[i] * x[j] for s, (i, j) in zip(sums, both)]
        second = [s + x[i] * y[j] for s, (i, j) in zip(sums[len(both) :], both)]
        return tuple(first + second)

    sums = lax.fori_loop(0, blocks // 8, step, (zero,) * (2 * len(both)))
    for k, s in enumerate(sums):
        o_ref[pl.ds(8 * k, 8), :] = s


def divide_kernel(t_ref, hi_ref, lo_ref):
    t = t_ref[...]
    hi = t.astype(BF16)
    hi_ref[...] = hi
    lo_ref[...] = (t - hi.astype(F32)).astype(BF16)


def divide(tiles):
    slots, width, _ = tiles.shape
    step = max(s for s in (1, 2, 4, 8) if slots % s == 0)
    spec = pl.BlockSpec((step, width, width), lambda i: (i, 0, 0))
    shape = jax.ShapeDtypeStruct(tiles.shape, BF16)
    return call(
        divide_kernel, (shape, shape), (tiles,), [spec], 8,
        flops=tiles.size * 4, grid=(slots // step,), out_specs=(spec, spec),
    )


def pick_kernel(vectors, slots, where_ref, at_ref, *refs):
    pieces, outs = refs[:-2], refs[-2:]
    for which, out in enumerate(outs):

        @pl.loop(0, slots, unroll=4)
        def _(t):
            m = where_ref[which, t]
            at = at_ref[which, t]
            value = jnp.zeros((vectors, out.shape[-1]), F32)
            for k, piece in enumerate(pieces):
                value = jnp.where(m == k, piece[pl.ds(at, vectors), :], value)
            out[pl.ds(t * vectors, vectors), :] = value


def multiply_kernel(vectors, step, transposed, x_ref, hi_ref, lo_ref, o_ref):
    base = pl.program_id(0) * step
    width = x_ref.shape[-1]
    dims = (((1,), (1 if transposed else 0,)), ((), ()))

    def left(t):
        x = x_ref[pl.ds(t * vectors, vectors), :]
        x = jnp.concatenate([x, jnp.zeros((8 - vectors, width), F32)], axis=0)
        hi = x.astype(BF16).astype(F32)
        lo = x - hi
        top = jnp.concatenate([hi, hi], axis=1)
        low = jnp.concatenate([lo, jnp.zeros_like(lo)], axis=1)
        return [top, low]

    @pl.loop(0, step // 2, unroll=step // 2)
    def _(p):
        i = 2 * p
        x = jnp.concatenate(left(base + i) + left(base + i + 1), axis=0).astype(BF16)
        along, across = (1, 0) if transposed else (0, 1)
        t = [jnp.concatenate([hi_ref[i + k], lo_ref[i + k]], axis=along) for k in (0, 1)]
        y = lax.dot_general(x, jnp.concatenate(t, axis=across), dims, preferred_element_type=F32)
        o_ref[pl.ds((base + i) * vectors, vectors), :] = (y[0:8, :width] + y[8:16, :width])[:vectors]
        o_ref[pl.ds((base + i + 1) * vectors, vectors), :] = (y[16:24, width:] + y[24:32, width:])[:vectors]


def multiply(x, high, low, ids, vectors, transposed, coupled=None):
    slots, width, _ = high.shape
    step = max(s for s in (2, 4, 8, 16, 20) if slots % s == 0)
    rows = vectors * slots
    spec = pl.BlockSpec((step, width, width), lambda i: (i, 0, 0))
    count = len(pairs(vectors))

    def kernel(x_ref, hi_ref, lo_ref, ids_ref, *refs):
        o_ref = refs[2] if coupled else refs[0]
        multiply_kernel(vectors, step, transposed, x_ref, hi_ref, lo_ref, o_ref)
        o_ref[pl.ds(rows, 8), :] = ids_ref[...]
        if coupled:

            @pl.when(pl.program_id(0) == pl.num_programs(0) - 1)
            def _():
                couple(vectors, slots, refs[0], o_ref, refs[1], refs[3], refs[4])

    out = jax.ShapeDtypeStruct((rows + 8, width), F32)
    if coupled:
        out = (out, jax.ShapeDtypeStruct((8, width), F32))
    operands = (x, high, low, ids) + (coupled or ())
    return call(
        kernel, out, operands, [VMEM, spec, spec] + [VMEM] * (len(operands) - 3), 12,
        flops=slots * 2 * 32 * 256 * 128, grid=(slots // step,),
        scratch=(pltpu.VMEM((-(-2 * count // 8) * 8, width), F32),) if coupled else (),
    )


def couple(vectors, slots, x_ref, y_ref, p_ref, o_ref, l_ref):
    both = pairs(vectors)
    n = len(both)
    lines, width = l_ref.shape

    def step(c, sums):
        at = pl.multiple_of(8 * c * vectors, 8)
        x = [x_ref[pl.ds(at + v, 8, stride=vectors), :] for v in range(vectors)]
        y = [y_ref[pl.ds(at + v, 8, stride=vectors), :] for v in range(vectors)]
        return tuple(s + (x[i] * y[j] + x[j] * y[i]) for s, (i, j) in zip(sums, both))

    sums = tuple(p_ref[pl.ds(8 * (n + k), 8), :] for k in range(n))
    sums = lax.fori_loop(0, slots // 8, step, sums)
    sums = [p_ref[pl.ds(8 * k, 8), :] for k in range(n)] + list(sums)
    for k, s in enumerate(sums):
        l_ref[k : k + 1, :] = jnp.sum(s, axis=0, keepdims=True)
    if lines > 2 * n:
        l_ref[2 * n :, :] = jnp.zeros((lines - 2 * n, width), F32)
    lane = lax.broadcasted_iota(jnp.int32, (8, width), 1)
    tile = jnp.zeros((8, width), F32)
    for g in range(lines // 8):
        part = jnp.sum(l_ref[pl.ds(8 * g, 8), :], axis=1, keepdims=True)
        tile = jnp.where(lane == g, part, tile)
    o_ref[...] = tile


def add_kernel(vectors, slots, blocks, started, me_ref, *refs):
    o_ref, lists = refs[-1], refs[:-1]
    if started:
        before, lists = lists[0], lists[1:]
    width = o_ref.shape[-1]
    row = lax.broadcasted_iota(jnp.int32, (blocks, width), 0) + me_ref[0] * blocks
    row = row.astype(F32)
    pad = jnp.zeros((width - slots, vectors * width), F32)
    sums = None
    for k in range(0, len(lists), 2):
        hots, blocks_of = [], []
        for ref in lists[k : k + 2]:
            ids = ref[vectors * slots : vectors * slots + 1, :]
            hots.append(jnp.where(ids == row, 1.0, 0.0).astype(BF16))
            y = [ref[pl.ds(v, slots, stride=vectors), :] for v in range(vectors)]
            blocks_of += [jnp.concatenate(y, axis=1), pad]
        hot = jnp.concatenate(hots, axis=1)
        y = jnp.concatenate(blocks_of, axis=0)
        hi = y.astype(BF16)
        lo = (y - hi.astype(F32)).astype(BF16)
        part = jnp.dot(hot, hi, preferred_element_type=F32) + jnp.dot(hot, lo, preferred_element_type=F32)
        sums = part if sums is None else sums + part
    for v in range(vectors):
        s = sums[:, v * width : (v + 1) * width]
        if started:
            s = s + before[pl.ds(v * blocks, blocks), :]
        o_ref[pl.ds(v * blocks, blocks), :] = s


def add_lists(me, lists, vectors, slots, blocks, before=None):
    width = lists[0].shape[-1]
    operands = (me,) + (() if before is None else (before,)) + tuple(lists)
    return call(
        functools.partial(add_kernel, vectors, slots, blocks, before is not None),
        jax.ShapeDtypeStruct((vectors * blocks, width), F32), operands,
        [SMEM] + [VMEM] * (len(operands) - 1), 16, flops=len(lists) * 2 * 256 * 256 * 768,
    )


def algebra(vectors, total, sums_ref):
    both = pairs(vectors)
    n = len(both)
    g, q = {}, {}
    for k, (i, j) in enumerate(both):
        g[i, j] = sums_ref[k : k + 1, :] * (1.0 / total)
        q[i, j] = q[j, i] = sums_ref[n + k : n + k + 1, :] * (1.0 / total)
    low, inv = {}, {}
    rev = []
    for j in range(vectors):
        s = g[j, j]
        for k in range(j):
            s = s - low[j, k] * low[j, k]
        rev.append(1.0 / jnp.sqrt(s))
        for i in range(j + 1, vectors):
            s = g[i, j]
            for k in range(j):
                s = s - low[i, k] * low[j, k]
            low[i, j] = s * rev[j]
    for j in range(vectors):
        inv[j, j] = rev[j]
        for i in range(j + 1, vectors):
            s = low[i, j] * inv[j, j]
            for k in range(j + 1, i):
                s = s + low[i, k] * inv[k, j]
            inv[i, j] = -s * rev[i]
    half, onto, proj = {}, {}, {}
    for i in range(vectors):
        for j in range(vectors):
            half[i, j] = sum(inv[i, k] * q[k, j] for k in range(i + 1))
    for i in range(vectors):
        for j in range(vectors):
            proj[i, j] = sum(half[i, k] * inv[j, k] for k in range(j + 1))
    for i in range(vectors):
        for j in range(vectors):
            onto[i, j] = sum(proj[i, k] * inv[k, j] for k in range(j, vectors))
    return inv, onto


def finish_kernel(vectors, total, steps, tile_ref, x_ref, d_ref, m_ref, final_ref, residual_ref, coef, res, fin, sums_ref):
    blocks, width = d_ref.shape
    chunk = blocks // steps
    start = pl.program_id(0) * chunk
    both = pairs(vectors)
    places = {("i", key): k for k, key in enumerate(both)}
    for i in range(vectors):
        for j in range(vectors):
            places["o", (i, j)] = len(places)

    @pl.when(pl.program_id(0) == 0)
    def _():
        for g in range(sums_ref.shape[0] // 8):
            sums_ref[pl.ds(8 * g, 8), :] = jnp.broadcast_to(tile_ref[:, g : g + 1], (8, width))
        inv, onto = algebra(vectors, total, sums_ref)
        for name, table in (("i", inv), ("o", onto)):
            for key in table:
                coef[pl.ds(8 * places[name, key], 8), :] = jnp.broadcast_to(table[key], (8, width))

    @pl.loop(0, chunk // 8, unroll=4)
    def _(c):
        local = pl.multiple_of(c * 8, 8)
        at = pl.multiple_of(start + local, 8)
        d = d_ref[pl.ds(at, 8), :]
        rd = 1.0 / d
        x = [x_ref[pl.ds(at * vectors + v, 8, stride=vectors), :] for v in range(vectors)]
        m = [m_ref[pl.ds(v * blocks + at, 8), :] + x[v] * d for v in range(vectors)]

        def value(name, i, j):
            return coef[pl.ds(8 * places[name, (i, j)], 8), :]

        for i in range(vectors):
            basis = r = None
            for j in range(i + 1):
                f = value("i", i, j)
                basis = f * x[j] if basis is None else basis + f * x[j]
                r = f * m[j] if r is None else r + f * m[j]
            for j in range(vectors):
                r = r - value("o", i, j) * x[j]
            res[pl.ds(8 * local + i, 8, stride=8), :] = r
            fin[pl.ds(8 * local + i, 8, stride=8), :] = basis - r * rd

    @pl.loop(0, chunk, unroll=8)
    def _(b):
        at = pl.multiple_of(b * width, width)
        residual_ref[:, pl.ds(at, width)] = res[pl.ds(pl.multiple_of(8 * b, 8), vectors), :]
        final_ref[:, pl.ds(at, width)] = fin[pl.ds(pl.multiple_of(8 * b, 8), vectors), :]


def body(start_block, diagonal, tile_values, tile_rows, tile_cols, tile_counts, offset_map):
    tiles = tile_values[0, 0]
    live_count = tile_counts[0, 0]
    row_size = lax.axis_size("row")
    off_size = lax.axis_size("off")
    me = lax.axis_index("off").astype(jnp.int32)
    offset = offset_map[me]
    vectors, shard = start_block.shape
    slots, width, _ = tiles.shape
    blocks = shard // width
    total = shard * off_size * row_size
    distances = range(row_size // 2)
    count = len(pairs(vectors))

    packed = call(
        functools.partial(pack_kernel, vectors, blocks),
        jax.ShapeDtypeStruct((vectors * blocks, width), F32), (start_block,),
    )
    live = jnp.arange(slots, dtype=jnp.int32) < live_count
    row_ids = jnp.where(live, tile_rows[0, 0], -1)
    col_ids = jnp.where(live, tile_cols[0, 0], -1)

    def padded(ids):
        return jnp.pad(ids.astype(F32)[None, :], ((0, 7), (0, width - slots)), constant_values=-1)

    row_line, col_line = padded(row_ids), padded(col_ids)
    group_line = lax.switch(
        offset,
        [functools.partial(lambda s, c: shift(c, s) if s else c, s) for s in distances],
        col_line,
    )
    both = jnp.stack([row_ids, group_line[0, :slots].astype(jnp.int32)])
    where = jnp.where(both < 0, -1, (both // blocks) ^ me)
    at = jnp.where(both < 0, 0, both % blocks) * vectors

    diagonal = diagonal.reshape(blocks, width)
    inner = call(
        functools.partial(inner_kernel, vectors),
        jax.ShapeDtypeStruct((16 * count, width), F32), (packed, diagonal),
    )
    high, low = divide(tiles)
    pieces = gather_off(packed, (where, at, inner, high, low))
    picked = jax.ShapeDtypeStruct((vectors * slots, width), F32)
    picked_row, picked_col = call(
        functools.partial(pick_kernel, vectors, slots), (picked, picked),
        (where, at, *pieces), [SMEM, SMEM] + [VMEM] * off_size,
    )

    row_bits, off_bits = bits_of("row")[::-1], bits_of("off")[::-1]

    def middle(s, picked_row, picked_col, high, low, row_line, col_line, inner):
        arrived = shift(picked_col, -s) if s else picked_col
        mirrored = multiply(picked_row, high, low, col_line, vectors, False)
        returned = shift(mirrored, s) if s else mirrored
        direct, sums = multiply(arrived, high, low, row_line, vectors, True, (picked_row, inner))
        return direct, returned, sums

    direct, returned, sums = lax.switch(
        offset,
        [functools.partial(middle, s) for s in distances],
        picked_row, picked_col, high, low, row_line, col_line, inner,
    )
    stages = [sums]
    order = [("off", off_bits[-1])] + [("row", b) for b in row_bits] + [("off", b) for b in off_bits[:-1]]
    for axis, bit in order[:-1]:
        stages.append(sum_step(stages[-1], axis, bit))
    lists = []
    for a, b in zip(gather_off(direct, (stages[-2],)), gather_off(returned, (stages[-1],))):
        lists += [a, b]
    half = off_size
    image = add_lists(me[None], lists[:half], vectors, slots, blocks)
    sums = sum_step(stages[-1], *order[-1])
    image = add_lists(me[None], lists[half:], vectors, slots, blocks, image)
    out = jax.ShapeDtypeStruct((vectors, shard), F32)
    steps = 2 if blocks % 64 == 0 else 1
    spec = pl.BlockSpec((vectors, shard // steps), lambda i: (0, i))
    return call(
        functools.partial(finish_kernel, vectors, float(total), steps), (out, out),
        (sums, packed, diagonal, image), limit=24,
        scratch=(
            pltpu.VMEM((8 * (vectors * vectors + count), width), F32),
            pltpu.VMEM((8 * blocks // steps, width), F32),
            pltpu.VMEM((8 * blocks // steps, width), F32),
            pltpu.VMEM((-(-2 * count // 8) * 8, width), F32),
        ),
        grid=(steps,), out_specs=(spec, spec),
    )


def solution(mesh):
    return jax.shard_map(
        body,
        mesh=mesh,
        in_specs=(
            P(None, ("row", "off")),
            P(("row", "off")),
            P("row", "off", None, None, None),
            P("row", "off", None),
            P("row", "off", None),
            P("row", "off"),
            P(),
        ),
        out_specs=(P(None, ("row", "off")), P(None, ("row", "off"))),
        check_vma=False,
    )
```

```python
import functools

import jax
import jax.numpy as jnp
from jax import lax
from jax.experimental import pallas as pl
from jax.experimental.pallas import tpu as pltpu
from jax.sharding import PartitionSpec as P


VMEM = pl.BlockSpec(memory_space=pltpu.VMEM)
SMEM = pl.BlockSpec(memory_space=pltpu.SMEM)
MIB = 1 << 20
BF16 = jnp.bfloat16
F32 = jnp.float32


def swap(x, axis, mask):
    n = lax.axis_size(axis)
    return lax.ppermute(x, axis, [(i, i ^ mask) for i in range(n)])


def shift(x, distance):
    n = lax.axis_size("row")
    return lax.ppermute(x, "row", [(i, (i + distance) % n) for i in range(n)])


def after(x, *others):
    return lax.optimization_barrier((x, *others))[0]


def bits_of(axis):
    return [1 << b for b in reversed(range(lax.axis_size(axis).bit_length() - 1))]


def gather_off(x, hold=()):
    pieces = {0: x}
    for bit in bits_of("off"):
        for m in list(pieces):
            source = after(pieces[m], *hold) if m and hold else pieces[m]
            pieces[m | bit] = swap(source, "off", bit)
    return [pieces[m] for m in sorted(pieces)]


def sum_step(x, axis, bit):
    return x + swap(x, axis, bit)


def pairs(vectors):
    return [(i, j) for i in range(vectors) for j in range(i + 1)]


def call(kernel, out_shape, operands, in_specs=None, limit=16, scratch=(), flops=0, **kw):
    many = isinstance(out_shape, tuple)
    moved = sum(x.size * x.dtype.itemsize for x in operands)
    return pl.pallas_call(
        kernel,
        out_shape=out_shape,
        in_specs=in_specs or [VMEM] * len(operands),
        out_specs=kw.pop("out_specs", (VMEM,) * len(out_shape) if many else VMEM),
        scratch_shapes=list(scratch),
        compiler_params=pltpu.CompilerParams(vmem_limit_bytes=limit * MIB),
        cost_estimate=pl.CostEstimate(flops=flops, bytes_accessed=moved, transcendentals=0),
        **kw,
    )(*operands)


def pack_kernel(vectors, blocks, x_ref, o_ref):
    width = o_ref.shape[-1]

    @pl.loop(0, blocks, unroll=8)
    def _(b):
        o_ref[pl.ds(b * vectors, vectors), :] = x_ref[:, pl.ds(pl.multiple_of(b * width, width), width)]


def inner_kernel(vectors, x_ref, d_ref, o_ref):
    blocks, width = d_ref.shape
    both = pairs(vectors)
    zero = jnp.zeros((8, width), F32)

    def step(c, sums):
        at = pl.multiple_of(c * 8, 8)
        d = d_ref[pl.ds(at, 8), :]
        x = [x_ref[pl.ds(at * vectors + v, 8, stride=vectors), :] for v in range(vectors)]
        y = [a * d for a in x]
        first = [s + x[i] * x[j] for s, (i, j) in zip(sums, both)]
        second = [s + x[i] * y[j] for s, (i, j) in zip(sums[len(both) :], both)]
        return tuple(first + second)

    sums = lax.fori_loop(0, blocks // 8, step, (zero,) * (2 * len(both)))
    for k, s in enumerate(sums):
        o_ref[pl.ds(8 * k, 8), :] = s


def divide_kernel(t_ref, hi_ref, lo_ref):
    t = t_ref[...]
    hi = t.astype(BF16)
    hi_ref[...] = hi
    lo_ref[...] = (t - hi.astype(F32)).astype(BF16)


def divide(tiles):
    slots, width, _ = tiles.shape
    step = max(s for s in (1, 2, 4, 8) if slots % s == 0)
    spec = pl.BlockSpec((step, width, width), lambda i: (i, 0, 0))
    shape = jax.ShapeDtypeStruct(tiles.shape, BF16)
    return call(
        divide_kernel, (shape, shape), (tiles,), [spec], 8,
        flops=tiles.size * 4, grid=(slots // step,), out_specs=(spec, spec),
    )


def pick_kernel(vectors, slots, where_ref, at_ref, *refs):
    pieces, outs = refs[:-2], refs[-2:]
    for which, out in enumerate(outs):

        @pl.loop(0, slots, unroll=16 if slots % 16 == 0 else 1)
        def _(t):
            m = where_ref[which, t]
            at = at_ref[which, t]
            value = jnp.zeros((vectors, out.shape[-1]), F32)
            for k, piece in enumerate(pieces):
                value = jnp.where(m == k, piece[pl.ds(at, vectors), :], value)
            out[pl.ds(t * vectors, vectors), :] = value


def multiply_kernel(vectors, step, transposed, x_ref, hi_ref, lo_ref, o_ref):
    base = pl.program_id(0) * step
    width = x_ref.shape[-1]
    dims = (((1,), (1 if transposed else 0,)), ((), ()))

    def left(t):
        x = x_ref[pl.ds(t * vectors, vectors), :]
        x = jnp.concatenate([x, jnp.zeros((8 - vectors, width), F32)], axis=0)
        hi = x.astype(BF16).astype(F32)
        lo = x - hi
        top = jnp.concatenate([hi, hi], axis=1)
        low = jnp.concatenate([lo, jnp.zeros_like(lo)], axis=1)
        return [top, low]

    @pl.loop(0, step // 2, unroll=step // 2)
    def _(p):
        i = 2 * p
        x = jnp.concatenate(left(base + i) + left(base + i + 1), axis=0).astype(BF16)
        along, across = (1, 0) if transposed else (0, 1)
        t = [jnp.concatenate([hi_ref[i + k], lo_ref[i + k]], axis=along) for k in (0, 1)]
        y = lax.dot_general(x, jnp.concatenate(t, axis=across), dims, preferred_element_type=F32)
        o_ref[pl.ds((base + i) * vectors, vectors), :] = (y[0:8, :width] + y[8:16, :width])[:vectors]
        o_ref[pl.ds((base + i + 1) * vectors, vectors), :] = (y[16:24, width:] + y[24:32, width:])[:vectors]


def multiply(x, high, low, ids, vectors, transposed, coupled=None):
    slots, width, _ = high.shape
    step = max(s for s in (2, 4, 8, 16, 20) if slots % s == 0)
    rows = vectors * slots
    spec = pl.BlockSpec((step, width, width), lambda i: (i, 0, 0))
    count = len(pairs(vectors))

    def kernel(x_ref, hi_ref, lo_ref, ids_ref, *refs):
        o_ref = refs[2] if coupled else refs[0]
        multiply_kernel(vectors, step, transposed, x_ref, hi_ref, lo_ref, o_ref)
        o_ref[pl.ds(rows, 8), :] = ids_ref[...]
        if coupled:

            @pl.when(pl.program_id(0) == pl.num_programs(0) - 1)
            def _():
                couple(vectors, slots, refs[0], o_ref, refs[1], refs[3], refs[4])

    out = jax.ShapeDtypeStruct((rows + 8, width), F32)
    if coupled:
        out = (out, jax.ShapeDtypeStruct((8, width), F32))
    operands = (x, high, low, ids) + (coupled or ())
    return call(
        kernel, out, operands, [VMEM, spec, spec] + [VMEM] * (len(operands) - 3), 12,
        flops=slots * 2 * 32 * 256 * 128, grid=(slots // step,),
        scratch=(pltpu.VMEM((-(-2 * count // 8) * 8, width), F32),) if coupled else (),
    )


def couple(vectors, slots, x_ref, y_ref, p_ref, o_ref, l_ref):
    both = pairs(vectors)
    n = len(both)
    lines, width = l_ref.shape

    def step(c, sums):
        at = pl.multiple_of(8 * c * vectors, 8)
        x = [x_ref[pl.ds(at + v, 8, stride=vectors), :] for v in range(vectors)]
        y = [y_ref[pl.ds(at + v, 8, stride=vectors), :] for v in range(vectors)]
        return tuple(s + (x[i] * y[j] + x[j] * y[i]) for s, (i, j) in zip(sums, both))

    sums = tuple(p_ref[pl.ds(8 * (n + k), 8), :] for k in range(n))
    sums = lax.fori_loop(0, slots // 8, step, sums)
    sums = [p_ref[pl.ds(8 * k, 8), :] for k in range(n)] + list(sums)
    for k, s in enumerate(sums):
        l_ref[k : k + 1, :] = jnp.sum(s, axis=0, keepdims=True)
    if lines > 2 * n:
        l_ref[2 * n :, :] = jnp.zeros((lines - 2 * n, width), F32)
    lane = lax.broadcasted_iota(jnp.int32, (8, width), 1)
    tile = jnp.zeros((8, width), F32)
    for g in range(lines // 8):
        part = jnp.sum(l_ref[pl.ds(8 * g, 8), :], axis=1, keepdims=True)
        tile = jnp.where(lane == g, part, tile)
    o_ref[...] = tile


def add_kernel(vectors, slots, blocks, started, me_ref, *refs):
    o_ref, lists = refs[-1], refs[:-1]
    if started:
        before, lists = lists[0], lists[1:]
    width = o_ref.shape[-1]
    row = lax.broadcasted_iota(jnp.int32, (blocks, width), 0) + me_ref[0] * blocks
    row = row.astype(F32)
    pad = jnp.zeros((width - slots, vectors * width), F32)
    sums = None
    for k in range(0, len(lists), 2):
        hots, blocks_of = [], []
        for ref in lists[k : k + 2]:
            ids = ref[vectors * slots : vectors * slots + 1, :]
            hots.append(jnp.where(ids == row, 1.0, 0.0).astype(BF16))
            y = [ref[pl.ds(v, slots, stride=vectors), :] for v in range(vectors)]
            blocks_of += [jnp.concatenate(y, axis=1), pad]
        hot = jnp.concatenate(hots, axis=1)
        y = jnp.concatenate(blocks_of, axis=0)
        hi = y.astype(BF16)
        lo = (y - hi.astype(F32)).astype(BF16)
        part = jnp.dot(hot, hi, preferred_element_type=F32) + jnp.dot(hot, lo, preferred_element_type=F32)
        sums = part if sums is None else sums + part
    for v in range(vectors):
        s = sums[:, v * width : (v + 1) * width]
        if started:
            s = s + before[pl.ds(v * blocks, blocks), :]
        o_ref[pl.ds(v * blocks, blocks), :] = s


def add_lists(me, lists, vectors, slots, blocks, before=None):
    width = lists[0].shape[-1]
    operands = (me,) + (() if before is None else (before,)) + tuple(lists)
    return call(
        functools.partial(add_kernel, vectors, slots, blocks, before is not None),
        jax.ShapeDtypeStruct((vectors * blocks, width), F32), operands,
        [SMEM] + [VMEM] * (len(operands) - 1), 16, flops=len(lists) * 2 * 256 * 256 * 768,
    )


def algebra(vectors, total, sums_ref):
    both = pairs(vectors)
    n = len(both)
    g, q = {}, {}
    for k, (i, j) in enumerate(both):
        g[i, j] = sums_ref[k : k + 1, :] * (1.0 / total)
        q[i, j] = q[j, i] = sums_ref[n + k : n + k + 1, :] * (1.0 / total)
    low, inv = {}, {}
    rev = []
    for j in range(vectors):
        s = g[j, j]
        for k in range(j):
            s = s - low[j, k] * low[j, k]
        rev.append(1.0 / jnp.sqrt(s))
        for i in range(j + 1, vectors):
            s = g[i, j]
            for k in range(j):
                s = s - low[i, k] * low[j, k]
            low[i, j] = s * rev[j]
    for j in range(vectors):
        inv[j, j] = rev[j]
        for i in range(j + 1, vectors):
            s = low[i, j] * inv[j, j]
            for k in range(j + 1, i):
                s = s + low[i, k] * inv[k, j]
            inv[i, j] = -s * rev[i]
    half, onto, proj = {}, {}, {}
    for i in range(vectors):
        for j in range(vectors):
            half[i, j] = sum(inv[i, k] * q[k, j] for k in range(i + 1))
    for i in range(vectors):
        for j in range(vectors):
            proj[i, j] = sum(half[i, k] * inv[j, k] for k in range(j + 1))
    for i in range(vectors):
        for j in range(vectors):
            onto[i, j] = sum(proj[i, k] * inv[k, j] for k in range(j, vectors))
    return inv, onto


def finish_kernel(vectors, total, steps, tile_ref, x_ref, d_ref, m_ref, final_ref, residual_ref, coef, res, fin, sums_ref):
    blocks, width = d_ref.shape
    chunk = blocks // steps
    start = pl.program_id(0) * chunk
    both = pairs(vectors)
    places = {("i", key): k for k, key in enumerate(both)}
    for i in range(vectors):
        for j in range(vectors):
            places["o", (i, j)] = len(places)

    @pl.when(pl.program_id(0) == 0)
    def _():
        for g in range(sums_ref.shape[0] // 8):
            sums_ref[pl.ds(8 * g, 8), :] = jnp.broadcast_to(tile_ref[:, g : g + 1], (8, width))
        inv, onto = algebra(vectors, total, sums_ref)
        for name, table in (("i", inv), ("o", onto)):
            for key in table:
                coef[pl.ds(8 * places[name, key], 8), :] = jnp.broadcast_to(table[key], (8, width))

    @pl.loop(0, chunk // 8, unroll=8 if chunk % 64 == 0 else 1)
    def _(c):
        local = pl.multiple_of(c * 8, 8)
        at = pl.multiple_of(start + local, 8)
        d = d_ref[pl.ds(at, 8), :]
        rd = 1.0 / d
        x = [x_ref[pl.ds(at * vectors + v, 8, stride=vectors), :] for v in range(vectors)]
        m = [m_ref[pl.ds(v * blocks + at, 8), :] + x[v] * d for v in range(vectors)]

        def value(name, i, j):
            return coef[pl.ds(8 * places[name, (i, j)], 8), :]

        for i in range(vectors):
            basis = r = None
            for j in range(i + 1):
                f = value("i", i, j)
                basis = f * x[j] if basis is None else basis + f * x[j]
                r = f * m[j] if r is None else r + f * m[j]
            for j in range(vectors):
                r = r - value("o", i, j) * x[j]
            res[pl.ds(8 * local + i, 8, stride=8), :] = r
            fin[pl.ds(8 * local + i, 8, stride=8), :] = basis - r * rd

    @pl.loop(0, chunk, unroll=16)
    def _(b):
        at = pl.multiple_of(b * width, width)
        residual_ref[:, pl.ds(at, width)] = res[pl.ds(pl.multiple_of(8 * b, 8), vectors), :]
        final_ref[:, pl.ds(at, width)] = fin[pl.ds(pl.multiple_of(8 * b, 8), vectors), :]


def body(start_block, diagonal, tile_values, tile_rows, tile_cols, tile_counts, offset_map):
    tiles = tile_values[0, 0]
    live_count = tile_counts[0, 0]
    row_size = lax.axis_size("row")
    off_size = lax.axis_size("off")
    me = lax.axis_index("off").astype(jnp.int32)
    offset = offset_map[me]
    vectors, shard = start_block.shape
    slots, width, _ = tiles.shape
    blocks = shard // width
    total = shard * off_size * row_size
    distances = range(row_size // 2)
    count = len(pairs(vectors))

    packed = call(
        functools.partial(pack_kernel, vectors, blocks),
        jax.ShapeDtypeStruct((vectors * blocks, width), F32), (start_block,),
    )
    live = jnp.arange(slots, dtype=jnp.int32) < live_count
    row_ids = jnp.where(live, tile_rows[0, 0], -1)
    col_ids = jnp.where(live, tile_cols[0, 0], -1)

    def padded(ids):
        return jnp.pad(ids.astype(F32)[None, :], ((0, 7), (0, width - slots)), constant_values=-1)

    row_line, col_line = padded(row_ids), padded(col_ids)

    def routed(function, *operands):
        if len(distances) <= 4:

            def branch(s):
                return functools.partial(function, lambda x, sign: shift(x, sign * s) if s else x)

            return lax.switch(offset, [branch(s) for s in distances], *operands)

        def move(x, sign):
            for b in range((len(distances) - 1).bit_length()):
                x = jnp.where(offset >> b & 1 == 1, shift(x, sign << b), x)
            return x

        return function(move, *operands)

    group_line = routed(lambda move, line: move(line, 1), col_line)
    both = jnp.stack([row_ids, group_line[0, :slots].astype(jnp.int32)])
    where = jnp.where(both < 0, -1, (both // blocks) ^ me)
    at = jnp.where(both < 0, 0, both % blocks) * vectors

    diagonal = diagonal.reshape(blocks, width)
    inner = call(
        functools.partial(inner_kernel, vectors),
        jax.ShapeDtypeStruct((16 * count, width), F32), (packed, diagonal),
    )
    high, low = divide(tiles)
    pieces = gather_off(packed, (where, at, inner, high, low))
    picked = jax.ShapeDtypeStruct((vectors * slots, width), F32)
    picked_row, picked_col = call(
        functools.partial(pick_kernel, vectors, slots), (picked, picked),
        (where, at, *pieces), [SMEM, SMEM] + [VMEM] * off_size,
    )

    row_bits, off_bits = bits_of("row")[::-1], bits_of("off")[::-1]

    def middle(move, picked_row, picked_col, high, low, row_line, col_line, inner):
        arrived = move(picked_col, -1)
        mirrored = multiply(picked_row, high, low, col_line, vectors, False)
        returned = move(mirrored, 1)
        direct, sums = multiply(arrived, high, low, row_line, vectors, True, (picked_row, inner))
        return direct, returned, sums

    direct, returned, sums = routed(
        middle, picked_row, picked_col, high, low, row_line, col_line, inner
    )
    stages = [sums]
    order = [("off", off_bits[-1])] + [("row", b) for b in row_bits] + [("off", b) for b in off_bits[:-1]]
    for axis, bit in order[:-1]:
        stages.append(sum_step(stages[-1], axis, bit))
    lists = []
    for a, b in zip(gather_off(direct, (stages[-2],)), gather_off(returned, (stages[-2],))):
        lists += [a, b]
    half = off_size
    image = add_lists(me[None], lists[:half], vectors, slots, blocks)
    sums = sum_step(stages[-1], *order[-1])
    image = add_lists(me[None], lists[half:], vectors, slots, blocks, image)
    out = jax.ShapeDtypeStruct((vectors, shard), F32)
    steps = 2 if blocks % 64 == 0 else 1
    spec = pl.BlockSpec((vectors, shard // steps), lambda i: (0, i))
    return call(
        functools.partial(finish_kernel, vectors, float(total), steps), (out, out),
        (sums, packed, diagonal, image), limit=24,
        scratch=(
            pltpu.VMEM((8 * (vectors * vectors + count), width), F32),
            pltpu.VMEM((8 * blocks // steps, width), F32),
            pltpu.VMEM((8 * blocks // steps, width), F32),
            pltpu.VMEM((-(-2 * count // 8) * 8, width), F32),
        ),
        grid=(steps,), out_specs=(spec, spec),
    )


def solution(mesh):
    return jax.shard_map(
        body,
        mesh=mesh,
        in_specs=(
            P(None, ("row", "off")),
            P(("row", "off")),
            P("row", "off", None, None, None),
            P("row", "off", None),
            P("row", "off", None),
            P("row", "off"),
            P(),
        ),
        out_specs=(P(None, ("row", "off")), P(None, ("row", "off"))),
        check_vma=False,
    )
```
